32 devices in a mesh: row: 2 (over core), col: 2 (over x), depth: 8 (over z, y).
Axes of the slice: x: 2, y: 2, z: 4, core: 2. Of those that a mesh axis runs over, the one named last changes fastest.
Arguments:
- a_blocks: bfloat16 [64, 128, 4096], P('row', ('col', 'depth')), may hold values from -6 to 6
- a_mask: int32 [64, 128], P('row', ('col', 'depth')), may hold values 0 or 1
- a_row_ids: int32 [64], replicated, may hold values from 0 to 63, as said below
- a_col_ids: int32 [128], replicated, may hold values from 0 to 127, as said below
- b_matrix: bfloat16 [8192, 6144], P(('row', 'depth'), 'col'), may hold values from -0.0625 to 0.0625
- b_mask: int32 [128, 96], P(('row', 'depth'), 'col'), may hold values 0 or 1
Outputs:
- product: bfloat16 [4096, 6144], P(('row', 'depth'), 'col')
The draws below stay inside these ranges and needn't reach their ends.
Inputs may be any that keep to these rules, and one draw needn't show every extreme that they name: `a_row_ids`: A permutation of the block rows; each aligned set of 32 entries holds at most 17 block rows r with the same r // 32, and every draw reaches 17. `a_col_ids`: A permutation of the block columns; entry v holds a block column k with (k // 8) % 8 == (v // 8) % 8.
All inputs are finite; a program needn't handle non-finite values. No bound on the sum of `a_mask` or of `b_mask` on one device may be relied on, other than what follows from the above.
Results may differ from the reference program's by a relative error of at most 0.001.
Values may be sent and summed in bfloat16 or wider, within the bound.
No kernel may reach another device: no remote copies, remote signals or barrier semaphores. Data moves between devices by JAX's collectives and lax.ppermute only.
A program may use at most 128 MiB of HBM per device.

```python
import jax
import jax.numpy as jnp
from jax import lax

BLOCK = 64
BAS = 8192
NV = 6144
ROWS = 4096
NBR = 64
RB = 32
KBLK = 128
KC = 8


def draw_a_row_ids(key, part):
    grid_size = NBR // RB
    spread = RB // grid_size
    first_key, second_key, third_key = jax.random.split(key, 3)
    gaining = jax.random.permutation(first_key, grid_size).astype(jnp.int32)
    losing = jnp.roll(gaining, -1)
    positions = jnp.arange(RB, dtype=jnp.int32)
    labels = jnp.where(positions[None, :] == losing[:, None] * spread, gaining[:, None], (positions // spread)[None, :])
    mixing = jax.vmap(lambda single: jax.random.permutation(single, RB))(jax.random.split(second_key, grid_size)).astype(jnp.int32)
    labels = jnp.take_along_axis(labels, mixing, axis=1).reshape(-1)
    tiebreak = jax.random.permutation(third_key, NBR).astype(jnp.int32)
    ranking = jnp.argsort(labels * NBR + tiebreak, stable=True).astype(jnp.int32)
    return jnp.zeros((NBR,), jnp.int32).at[ranking].set(jnp.arange(NBR, dtype=jnp.int32))


def draw_a_col_ids(key, part):
    grid_size = NBR // RB
    planes = KBLK // (KC * grid_size)
    members = grid_size * KC
    first_key, second_key = jax.random.split(key, 2)
    shuffles = jax.vmap(lambda single: jax.random.permutation(single, members))(jax.random.split(first_key, planes)).astype(jnp.int32)
    chosen = jax.random.randint(second_key, (), 0, planes)
    shuffles = jnp.where(jnp.arange(planes, dtype=jnp.int32)[:, None] == chosen, jnp.arange(members, dtype=jnp.int32)[None, :], shuffles)
    column = jnp.arange(KBLK, dtype=jnp.int32)
    shard_of = column // KC
    plane_of = shard_of % planes
    holder = shard_of // planes
    picked = shuffles[plane_of, holder * KC + column % KC]
    return ((picked // KC * planes + plane_of) * KC + picked % KC).astype(jnp.int32)


def plant(entries, rng, least, high):
    shape = entries.shape
    place = [jax.random.randint(jax.random.fold_in(rng, axis), (), 0, shape[axis]) for axis in range(len(shape))]
    entries = entries.at[tuple(place)].set(least)
    longest = shape.index(max(shape))
    place[longest] = (place[longest] + 1) % shape[longest]
    return entries.at[tuple(place)].set(high)


def levels(rng, shape, cuts, smallest, top_value):
    factor_of = 1.0
    for axis_at, shards_of in cuts:
        steps = jax.random.uniform(jax.random.fold_in(jax.random.fold_in(rng, 6), axis_at), (shards_of,), jnp.float32, smallest / len(cuts), top_value / len(cuts))
        factor_of = factor_of * jnp.repeat(jnp.exp(steps), shape[axis_at] // shards_of).reshape((-1,) + (1,) * (len(shape) - 1 - axis_at))
    return factor_of


def noise(rng, dims, scale, bound, cuts=(), held_as=jnp.bfloat16):
    loudness = levels(rng, dims, cuts, -0.22, 0.18) if cuts else 1.0
    entries = jax.random.normal(rng, dims, jnp.float32) * scale * loudness
    return jnp.minimum(jnp.maximum(entries, -bound), bound).astype(held_as)


def setup_inputs(seed: int = 0) -> dict:
    splits = jax.random.split(jax.random.key(seed), 7)
    a_blocks = noise(splits[0], (NBR, KBLK, BLOCK * BLOCK), 1.0, 6.0, ((0, 2), (1, 16)))
    a_mask = plant((jax.random.randint(splits[1], (NBR, KBLK), 0, 4) < 3).astype(jnp.int32), jax.random.fold_in(splits[1], 1), 0, 1)
    a_row_ids = draw_a_row_ids(jax.random.fold_in(splits[6], 71), 0)
    a_col_ids = draw_a_col_ids(jax.random.fold_in(splits[6], 71), 0)
    b_matrix = noise(splits[4], (BAS, NV), BAS ** -0.5, 0.0625, ((0, 16), (1, 2)))
    b_mask = plant((jax.random.randint(splits[5], (KBLK, NV // BLOCK), 0, 4) < 3).astype(jnp.int32), jax.random.fold_in(splits[5], 1), 0, 1)
    return {"a_blocks": a_blocks, "a_mask": a_mask, "a_row_ids": a_row_ids, "a_col_ids": a_col_ids, "b_matrix": b_matrix, "b_mask": b_mask}


def reference(a_blocks, a_mask, a_row_ids, a_col_ids, b_matrix, b_mask):
    row_slot = jnp.zeros((NBR,), jnp.int32).at[a_row_ids].set(jnp.arange(NBR, dtype=jnp.int32))
    col_slot = jnp.zeros((KBLK,), jnp.int32).at[a_col_ids].set(jnp.arange(KBLK, dtype=jnp.int32))
    masked = a_blocks * a_mask[:, :, None].astype(a_blocks.dtype)
    ordered = masked[row_slot][:, col_slot]
    left_matrix = ordered.reshape(NBR, KBLK, BLOCK, BLOCK).transpose(0, 2, 1, 3).reshape(ROWS, BAS)
    right_matrix = b_matrix.reshape(KBLK, BLOCK, NV // BLOCK, BLOCK) * b_mask[:, None, :, None].astype(b_matrix.dtype)
    right_matrix = right_matrix.reshape(BAS, NV)
    product = jnp.dot(left_matrix.astype(jnp.float32), right_matrix.astype(jnp.float32), precision=lax.Precision.HIGHEST)
    return product.astype(jnp.bfloat16)
```

```python
import functools
import math

import jax
import jax.numpy as jnp
from jax import lax
from jax.experimental import pallas as pl
from jax.experimental.pallas import tpu as pltpu
from jax.sharding import PartitionSpec as P

LINE = 4
CHUNKS = (4, 4, 4, 4)
PARTS = ((0, 1, 2, 3),)
SPAN = 32760.0
PAD = 16


def shifted(value, axis, offset):
    size = lax.axis_size(axis)
    return lax.ppermute(value, axis, [((i + offset) % size, i) for i in range(size)])


def member(value, near, offset):
    planes = lax.axis_size("depth") // near
    pairs = [
        (z * near + (y + offset) % near, z * near + y) for z in range(planes) for y in range(near)
    ]
    return lax.ppermute(value, "depth", pairs)


def hop(value, near, steps):
    pairs = [(a * near + y, b * near + y) for a, b in steps for y in range(near)]
    return lax.ppermute(value, "depth", pairs)


def edge_in(last):
    return ((0, 1), (last, last - 1))


def across(last):
    return ((1, last - 1), (last - 1, 1))


def edge_out(last):
    return ((1, 0), (last - 1, last))


def encode(total):
    peak = jnp.max(jnp.abs(total), axis=0, keepdims=True)
    level = jnp.ceil(jnp.log2(jnp.maximum(peak, 1e-30)) * 16.0)
    scaled = total * (jnp.exp2(level * (-1.0 / 16.0)) * SPAN)
    whole = (scaled + jnp.where(scaled >= 0.0, 0.5, -0.5)).astype(jnp.int32)
    return whole.astype(jnp.int16), level


def put_code(ref, cols, total):
    code, level = encode(total)
    rows = total.shape[0]
    ref[0:rows, cols] = code
    ref[rows : rows + PAD, cols] = (
        jnp.broadcast_to(level, (PAD, level.shape[1])).astype(jnp.int32).astype(jnp.int16)
    )


def decode(ref, cols, rows):
    level = ref[rows : rows + PAD, cols].astype(jnp.int32).astype(jnp.float32)[0:1]
    return ref[0:rows, cols].astype(jnp.int32).astype(jnp.float32) * (
        jnp.exp2(level * (1.0 / 16.0)) * (1.0 / SPAN)
    )


def col_tiles(width):
    step = 384 if width % 384 == 0 else 256 if width % 256 == 0 else 128
    return [slice(i, i + step) for i in range(0, width, step)]


def pick_kernel(grid, groups, home_rows, planes_y, offset, *refs):
    meta, inverse = refs[0], refs[1]
    masks = refs[2 : 2 + grid]
    raws = refs[2 + grid : 2 + 2 * grid]
    out = refs[2 + 2 * grid]
    held, sems = refs[3 + 2 * grid :]
    rows_dev, cols_dev = raws[0].shape[0], raws[0].shape[1]
    my_row, my_line, my_near, depth = meta[0], meta[2], meta[3], meta[4]
    near = lax.rem(my_near - offset + planes_y, planes_y)
    total = len(groups) * home_rows
    low = lax.broadcasted_iota(jnp.int32, (1, 128), 1) < 64

    def place(t):
        g = groups[0] + t // home_rows
        line = jnp.where(my_line < LINE // 2, LINE - 1 - g, g)
        block = (my_row * depth + line * planes_y + near) * home_rows + lax.rem(t, home_rows)
        slot = inverse[block]
        owner = lax.rem(slot // rows_dev - my_row + grid, grid)
        return owner, lax.rem(slot, rows_dev)

    def fetch(t, carry):
        owner, slot = place(t)
        for o in range(grid):
            @pl.when(owner == o)
            def _():
                pltpu.make_async_copy(raws[o].at[slot], held.at[t], sems.at[t]).start()
        return carry

    lax.fori_loop(0, total, fetch, 0)

    def lay(t, carry):
        owner, slot = place(t)
        pltpu.make_async_copy(raws[0].at[0], held.at[t], sems.at[t]).wait()
        x = held[t].reshape(cols_dev, 32, 128)
        for p in range(cols_dev // 2):
            keep = []
            for w in (2 * p, 2 * p + 1):
                flag = masks[0][slot, w]
                for o in range(1, grid):
                    flag = jnp.where(owner == o, masks[o][slot, w], flag)
                keep.append(flag)
            live = jnp.where(low, keep[0], keep[1]).astype(jnp.float32)
            a, b = x[2 * p].astype(jnp.float32), x[2 * p + 1].astype(jnp.float32)
            turned_a, turned_b = pltpu.roll(a, 64, 1), pltpu.roll(b, 64, 1)
            even = jnp.where(low, a, turned_b) * live
            odd = jnp.where(low, turned_a, b) * live
            pair = jnp.stack([even, odd], axis=1).reshape(64, 128).astype(jnp.bfloat16)
            out[pl.ds(pl.multiple_of(t * 64, 64), 64), p * 128 : (p + 1) * 128] = pair
        return carry

    lax.fori_loop(0, total, lay, 0)


def pick(meta, inverse, masks, raws, groups, home_rows, planes_y, offset):
    grid = len(raws)
    rows_dev, cols_dev, side2 = raws[0].shape
    total = len(groups) * home_rows
    width = cols_dev * 64
    smem = pl.BlockSpec(memory_space=pltpu.SMEM)
    return pl.pallas_call(
        functools.partial(pick_kernel, grid, groups, home_rows, planes_y, offset),
        out_shape=jax.ShapeDtypeStruct((total * 64, width), jnp.bfloat16),
        in_specs=[smem] * (2 + grid) + [pl.BlockSpec(memory_space=pl.ANY)] * grid,
        out_specs=pl.BlockSpec(memory_space=pltpu.VMEM),
        scratch_shapes=[
            pltpu.VMEM((total, cols_dev, side2), jnp.bfloat16),
            pltpu.SemaphoreType.DMA((total,)),
        ],
        cost_estimate=pl.CostEstimate(
            flops=0, transcendentals=0, bytes_accessed=4 * total * cols_dev * side2
        ),
        name=f"pick_{offset}_{groups[0]}",
    )(meta, inverse, *masks, *raws)


def cut_kernel(widths, mask, b, *outs):
    blocks = mask.shape[0]
    expand = (
        lax.broadcasted_iota(jnp.int32, (mask.shape[1], b.shape[1]), 1) // 64
        == lax.broadcasted_iota(jnp.int32, (mask.shape[1], b.shape[1]), 0)
    ).astype(jnp.float32)
    live = jnp.dot(
        mask[...].astype(jnp.float32), expand, preferred_element_type=jnp.float32
    )
    start = 0
    for out, width in zip(outs, widths):
        for s in range(blocks):
            rows = slice(s * 64, (s + 1) * 64)
            keep = live[s : s + 1, start : start + width].astype(jnp.bfloat16)
            out[rows, :] = b[rows, start : start + width] * keep
        start += width


def cut(b_matrix, b_mask, widths):
    vmem = pl.BlockSpec(memory_space=pltpu.VMEM)
    return pl.pallas_call(
        functools.partial(cut_kernel, widths),
        out_shape=[jax.ShapeDtypeStruct((b_matrix.shape[0], w), jnp.bfloat16) for w in widths],
        in_specs=[vmem, vmem],
        out_specs=[vmem] * len(widths),
        cost_estimate=pl.CostEstimate(
            flops=0, transcendentals=0, bytes_accessed=4 * b_matrix.size
        ),
        name="cut",
    )(b_mask, b_matrix)


def multiply_kernel(grid, planes_y, groups, coded, *refs):
    meta, col_ids = refs[0], refs[1]
    count = grid * planes_y
    lefts = refs[2 : 2 + count]
    rights = refs[2 + count : 2 + 2 * count]
    outs = refs[2 + 2 * count : -4]
    left, right, left_sems, right_sems = refs[-4:]
    sums, codes = outs[: len(groups)], outs[len(groups) :]
    piece = lefts[0].shape[1]
    cols_dev = piece // 64
    rows = left.shape[0] // len(groups)
    my_row, my_col, my_line, my_near, depth = meta[0], meta[1], meta[2], meta[3], meta[4]
    for x in range(grid):
        for y in range(planes_y):
            q = x * planes_y + y
            owner = lax.rem(my_col + x, grid) * depth + my_line * planes_y
            owner = owner + lax.rem(my_near + y, planes_y)
            for w in range(cols_dev):
                k = col_ids[owner * cols_dev + w]
                shift = lax.rem(k // (cols_dev * depth) - my_row + grid, grid)
                at = pl.multiple_of(lax.rem(k, cols_dev) * 64, 64)
                n = q * cols_dev + w
                for o in range(grid):
                    @pl.when(shift == o)
                    def _():
                        pltpu.make_async_copy(
                            rights[o * planes_y + y].at[pl.ds(at, 64)],
                            right.at[n * 64 : (n + 1) * 64],
                            right_sems.at[n],
                        ).start()
            pltpu.make_async_copy(
                lefts[q], left.at[:, q * piece : (q + 1) * piece], left_sems.at[q]
            ).start()
    for q in range(count):
        pltpu.make_async_copy(
            lefts[q], left.at[:, q * piece : (q + 1) * piece], left_sems.at[q]
        ).wait()
        for w in range(cols_dev):
            n = q * cols_dev + w
            pltpu.make_async_copy(
                rights[0].at[0:64], right.at[n * 64 : (n + 1) * 64], right_sems.at[n]
            ).wait()
    for i, g in enumerate(groups):
        for cols in col_tiles(right.shape[1]):
            total = jnp.dot(
                left[i * rows : (i + 1) * rows, :],
                right[:, cols],
                preferred_element_type=jnp.float32,
            )
            sums[i][:, cols] = total
            if g in coded:
                put_code(codes[coded.index(g)], cols, total)


def multiply(meta, col_ids, lefts, rights, groups, grid, planes_y):
    rows = lefts[0].shape[0] // len(groups)
    width = rights[0].shape[1]
    inner = lefts[0].shape[1] * len(lefts)
    coded = tuple(g for g in groups if g < LINE - 1)
    smem = pl.BlockSpec(memory_space=pltpu.SMEM)
    vmem = pl.BlockSpec(memory_space=pltpu.VMEM)
    outs = [jax.ShapeDtypeStruct((rows, width), jnp.float32) for _ in groups]
    outs += [jax.ShapeDtypeStruct((rows + PAD, width), jnp.int16) for _ in coded]
    got = pl.pallas_call(
        functools.partial(multiply_kernel, grid, planes_y, groups, coded),
        out_shape=outs,
        in_specs=[smem, smem] + [pl.BlockSpec(memory_space=pl.ANY)] * (len(lefts) + len(rights)),
        out_specs=[vmem] * len(outs),
        scratch_shapes=[
            pltpu.VMEM((lefts[0].shape[0], inner), jnp.bfloat16),
            pltpu.VMEM((inner, width), jnp.bfloat16),
            pltpu.SemaphoreType.DMA((len(lefts),)),
            pltpu.SemaphoreType.DMA((inner // 64,)),
        ],
        cost_estimate=pl.CostEstimate(
            flops=2 * lefts[0].shape[0] * inner * width,
            transcendentals=0,
            bytes_accessed=2 * inner * (lefts[0].shape[0] + width) + 6 * rows * width * len(groups),
        ),
        name=f"multiply_{groups[0]}",
    )(meta, col_ids, *lefts, *rights)
    sums = dict(zip(groups, got))
    codes = dict(zip(coded, got[len(groups) :]))
    return sums, codes


def relay_kernel(own, code, out):
    rows = own.shape[0]
    for cols in col_tiles(own.shape[1]):
        put_code(out, cols, own[:, cols] + decode(code, cols, rows))


def relay(own, code):
    vmem = pl.BlockSpec(memory_space=pltpu.VMEM)
    return pl.pallas_call(
        relay_kernel,
        out_shape=jax.ShapeDtypeStruct(code.shape, code.dtype),
        in_specs=[vmem, vmem],
        out_specs=vmem,
        cost_estimate=pl.CostEstimate(
            flops=0, transcendentals=0, bytes_accessed=8 * own.size
        ),
        name="relay",
    )(own, code)


def finish_kernel(start, meta, edge, inner, *refs):
    codes, out, stage, sem = refs[:3], refs[-3], refs[-2], refs[-1]
    rows = edge.shape[0]
    at_edge = jnp.logical_or(meta[2] == 0, meta[2] == LINE - 1)
    for cols in col_tiles(edge.shape[1]):
        total = jnp.where(at_edge, edge[:, cols], inner[:, cols])
        for code in codes:
            total = total + decode(code, cols, rows)
        stage[:, cols] = total.astype(jnp.bfloat16)
    copy = pltpu.make_async_copy(stage, out.at[:, start : start + edge.shape[1]], sem)
    copy.start()
    copy.wait()


def finish(meta, edge, inner, codes, start, full, so_far):
    vmem = pl.BlockSpec(memory_space=pltpu.VMEM)
    hbm = pl.BlockSpec(memory_space=pl.ANY)
    operands = [meta, edge, inner, *codes]
    specs = [pl.BlockSpec(memory_space=pltpu.SMEM)] + [vmem] * 5
    aliases = {}
    if so_far is not None:
        aliases = {len(operands): 0}
        operands.append(so_far)
        specs.append(hbm)
    return pl.pallas_call(
        functools.partial(finish_kernel, start),
        out_shape=jax.ShapeDtypeStruct((edge.shape[0], full), jnp.bfloat16),
        in_specs=specs,
        out_specs=hbm,
        scratch_shapes=[pltpu.VMEM(edge.shape, jnp.bfloat16), pltpu.SemaphoreType.DMA(())],
        input_output_aliases=aliases,
        cost_estimate=pl.CostEstimate(
            flops=0, transcendentals=0, bytes_accessed=16 * edge.size
        ),
        name="finish",
    )(*operands)


def body(a_blocks, a_mask, a_row_ids, a_col_ids, b_matrix, b_mask):
    grid = lax.axis_size("row")
    depth = lax.axis_size("depth")
    planes_y = depth // LINE
    last = LINE - 1
    rows_dev = a_blocks.shape[0]
    home_rows = rows_dev * grid // (grid * depth)
    full = b_matrix.shape[1]
    unit = full // sum(CHUNKS)
    widths = [unit * c for c in CHUNKS]

    slots = jnp.arange(8, dtype=jnp.int32)
    my_depth = lax.axis_index("depth")
    meta = jnp.zeros((8,), jnp.int32)
    for i, value in enumerate(
        (
            lax.axis_index("row"),
            lax.axis_index("col"),
            my_depth // planes_y,
            my_depth % planes_y,
            depth,
        )
    ):
        meta = jnp.where(slots == i, value, meta)
    stored = jnp.arange(a_row_ids.shape[0], dtype=jnp.int32)
    inverse = jnp.sum(
        jnp.where(a_row_ids[None, :] == stored[:, None], stored[None, :], 0), axis=1
    )

    raws = [a_blocks] + [shifted(a_blocks, "row", o) for o in range(1, grid)]
    masks = [a_mask] + [shifted(a_mask, "row", o) for o in range(1, grid)]
    cuts = cut(b_matrix, b_mask, widths)

    lefts = []
    for groups in PARTS:
        near = []
        for s in range(planes_y):
            picked = pick(meta, inverse, masks, raws, groups, home_rows, planes_y, s)
            near.append(member(picked, planes_y, s) if s else picked)
        far = [[shifted(v, "col", x) for v in near] for x in range(1, grid)]
        lefts.append(near + sum(far, []))

    product = None
    start = 0
    for width, mine in zip(widths, cuts):
        near = [mine] + [member(mine, planes_y, s) for s in range(1, planes_y)]
        rights = near + sum([[shifted(v, "row", o) for v in near] for o in range(1, grid)], [])
        sums, codes = {}, {}
        for groups, left in zip(PARTS, lefts):
            more, coded = multiply(meta, a_col_ids, left, rights, groups, grid, planes_y)
            sums.update(more)
            codes.update(coded)
        came = [hop(codes[g], planes_y, edge_in(last)) for g in range(LINE - 1)]
        crossed = [hop(relay(sums[g], came[g]), planes_y, across(last)) for g in range(2)]
        back = hop(relay(sums[3], crossed[0]), planes_y, edge_out(last))
        product = finish(
            meta, sums[3], sums[2], (came[2], crossed[1], back), start, full, product
        )
        start += width
    return product


def solution(mesh):
    return jax.shard_map(
        body,
        mesh=mesh,
        in_specs=(
            P("row", ("col", "depth"), None),
            P("row", ("col", "depth")),
            P(),
            P(),
            P(("row", "depth"), "col"),
            P(("row", "depth"), "col"),
        ),
        out_specs=P(("row", "depth"), "col"),
        check_vma=False,
    )
```

```python
import functools
import math

import jax
import jax.numpy as jnp
from jax import lax
from jax.experimental import pallas as pl
from jax.experimental.pallas import tpu as pltpu
from jax.sharding import PartitionSpec as P


LINE = 4
CHUNKS = (3, 3, 4, 2)
SPLIT = 2
DIRECT = 1
SPAN = 32760.0
PAD = 16
SHIFT = 16


def shifted(value, axis, offset):
    size = lax.axis_size(axis)
    return lax.ppermute(value, axis, [((i + offset) % size, i) for i in range(size)])


def member(value, near, offset):
    planes = lax.axis_size("depth") // near
    pairs = [
        (z * near + (y + offset) % near, z * near + y) for z in range(planes) for y in range(near)
    ]
    return lax.ppermute(value, "depth", pairs)


def hop(value, near, senders, flip):
    pairs = [(z * near + y, (z ^ flip) * near + y) for z in senders for y in range(near)]
    return lax.ppermute(value, "depth", pairs)


ALL = tuple(range(LINE))
EDGES = (0, LINE - 1)
INNER = tuple(range(1, LINE - 1))


def encode(total):
    peak = jnp.max(jnp.abs(total), axis=0, keepdims=True)
    level = jnp.ceil(jnp.log2(jnp.maximum(peak, 1e-30)) * 16.0)
    scaled = total * (jnp.exp2(level * (-1.0 / 16.0)) * SPAN)
    return jnp.round(scaled).astype(jnp.int32).astype(jnp.int16), level


def put_code(ref, at, cols, total):
    code, level = encode(total)
    rows = total.shape[0]
    ref[at : at + rows, cols] = code
    ref[at + rows : at + rows + PAD, cols] = (
        jnp.broadcast_to(level, (PAD, level.shape[1])).astype(jnp.int32).astype(jnp.int16)
    )


def decode(ref, at, cols, rows):
    level = ref[at + rows : at + rows + PAD, cols].astype(jnp.int32).astype(jnp.float32)[0:1]
    return ref[at : at + rows, cols].astype(jnp.int32).astype(jnp.float32) * (
        jnp.exp2(level * (1.0 / 16.0)) * (1.0 / SPAN)
    )


def tiled(width, fn):
    step = 256 if width % 256 == 0 else 128

    def run(n, carry):
        fn(pl.ds(pl.multiple_of(n * step, step), step))
        return carry

    lax.fori_loop(0, width // step, run, 0)


def pick_kernel(grid, groups, home_rows, planes_y, *refs):
    meta, inverse = refs[0], refs[1]
    masks = refs[2 : 2 + grid]
    choose = refs[2 + grid]
    raws = refs[3 + grid : 3 + 2 * grid]
    outs = refs[3 + 2 * grid : -2]
    held, sems = refs[-2:]
    rows_dev, cols_dev = raws[0].shape[0], raws[0].shape[1]
    my_row, my_line, my_near = meta[0], meta[2], meta[3]
    depth = LINE * planes_y
    count = len(groups) * home_rows
    batch = math.gcd(count, 4)

    def place(s, t):
        near = lax.rem(my_near - s + planes_y, planes_y)
        g = groups[0] + t // home_rows
        line = lax.bitwise_xor(my_line, LINE - 1 - g)
        block = (my_row * depth + line * planes_y + near) * home_rows + lax.rem(t, home_rows)
        slot = inverse[block]
        owner = lax.rem(lax.div(slot, rows_dev) - my_row + grid, grid)
        return owner, lax.rem(slot, rows_dev)

    def fetch(s):
        def run(t, carry):
            owner, slot = place(s, t)
            for o in range(grid):
                @pl.when(owner == o)
                def _():
                    n = s * count + t
                    pltpu.make_async_copy(raws[o].at[slot], held.at[n], sems.at[n]).start()
            return carry

        lax.fori_loop(0, count, run, 0)

    order = [*range(1, planes_y), 0]
    for s in order:
        fetch(s)
    low = lax.broadcasted_iota(jnp.int32, (64, 128), 1) < 64
    even = lax.broadcasted_iota(jnp.int32, (64, 128), 0) % 2 == 0
    same = low == even
    low_row = lax.broadcasted_iota(jnp.int32, (1, 128), 1) < 64

    def lay(s):
        def run(m, carry):
            stored = []
            for h in range(batch):
                n = s * count + m * batch + h
                pltpu.make_async_copy(raws[0].at[0], held.at[n], sems.at[n]).wait()
                x = held[n].astype(jnp.float32)
                parts = [x[:, 128 * i : 128 * (i + 1)] for i in range(32)]
                stored.append(jnp.concatenate(parts, axis=0).astype(jnp.bfloat16))
            spread = jnp.dot(
                choose[...],
                jnp.concatenate(stored, axis=1),
                preferred_element_type=jnp.float32,
            )
            for h in range(batch):
                t = m * batch + h
                owner, slot = place(s, t)
                for p in range(cols_dev // 2):
                    keep = []
                    for w in (2 * p, 2 * p + 1):
                        flag = masks[0][slot, w]
                        for o in range(1, grid):
                            flag = jnp.where(owner == o, masks[o][slot, w], flag)
                        keep.append(flag)
                    live = jnp.where(low_row, keep[0], keep[1]).astype(jnp.float32)
                    lanes = slice(128 * h, 128 * (h + 1))
                    first = spread[2 * p * 64 : (2 * p + 1) * 64, lanes]
                    second = spread[(2 * p + 1) * 64 : (2 * p + 2) * 64, lanes]
                    straight = jnp.where(low, first, second)
                    turned = pltpu.roll(jnp.where(low, second, first), 64, 1)
                    pair = jnp.where(same, straight, turned) * live
                    at = pl.ds(pl.multiple_of(t * 64, 64), 64)
                    outs[s][at, p * 128 : (p + 1) * 128] = pair.astype(jnp.bfloat16)
            return carry

        lax.fori_loop(0, count // batch, run, 0)

    for s in order:
        lay(s)


def pick(meta, inverse, masks, choose, raws, groups, home_rows, planes_y):
    grid = len(raws)
    cols_dev, side2 = raws[0].shape[1:]
    count = len(groups) * home_rows
    total = count * planes_y
    smem = pl.BlockSpec(memory_space=pltpu.SMEM)
    vmem = pl.BlockSpec(memory_space=pltpu.VMEM)
    shape = jax.ShapeDtypeStruct((count * 64, cols_dev * 64), jnp.bfloat16)
    return pl.pallas_call(
        functools.partial(pick_kernel, grid, groups, home_rows, planes_y),
        out_shape=[shape] * planes_y,
        in_specs=[smem] * (2 + grid) + [vmem] + [pl.BlockSpec(memory_space=pl.ANY)] * grid,
        out_specs=[vmem] * planes_y,
        scratch_shapes=[
            pltpu.VMEM((total, cols_dev, side2), jnp.bfloat16),
            pltpu.SemaphoreType.DMA((total,)),
        ],
        cost_estimate=pl.CostEstimate(
            flops=0, transcendentals=0, bytes_accessed=4 * total * cols_dev * side2
        ),
        name="pick",
    )(meta, inverse, *masks, choose, *raws)


def cut_kernel(widths, begin, wide, mask, b, *outs):
    blocks = mask.shape[0]
    shape = (mask.shape[1], b.shape[1])
    expand = (
        lax.broadcasted_iota(jnp.int32, shape, 1) // 64
        == lax.broadcasted_iota(jnp.int32, shape, 0)
    ).astype(jnp.float32)
    live = jnp.dot(
        mask[...].astype(jnp.float32), expand, preferred_element_type=jnp.float32
    ).astype(jnp.bfloat16)
    spans = [(sum(widths[:i]) + begin, w, outs[i]) for i, w in enumerate(widths)]
    if wide:
        spans = [(0, begin, None)] + spans
    for s in range(blocks):
        rows = slice(s * 64, (s + 1) * 64)
        for start, width, out in spans:
            cols = slice(start, start + width)
            kept = b[rows, cols] * live[s : s + 1, cols]
            if out is not None:
                out[rows, :] = kept
            if wide:
                outs[-1][rows, cols] = kept


def cut(b_matrix, b_mask, widths, begin, wide):
    vmem = pl.BlockSpec(memory_space=pltpu.VMEM)
    rows, full = b_matrix.shape
    read = full if wide else begin + sum(widths)
    outs = [*widths, full] if wide else widths

    def whole(shape):
        return pl.BlockSpec(shape, lambda i: (0, 0))

    return pl.pallas_call(
        functools.partial(cut_kernel, widths, begin, wide),
        grid=(1,),
        out_shape=[jax.ShapeDtypeStruct((rows, w), jnp.bfloat16) for w in outs],
        in_specs=[whole(b_mask.shape), whole((rows, read))],
        out_specs=[whole((rows, w)) for w in outs],
        cost_estimate=pl.CostEstimate(
            flops=0, transcendentals=0, bytes_accessed=6 * rows * read
        ),
        name="cut",
    )(b_mask, b_matrix)


def multiply_kernel(grid, planes_y, lows, direct, start, *refs):
    table = refs[0]
    count = grid * planes_y
    total_in = count * len(lows)
    lefts = [refs[1 + i * count : 1 + (i + 1) * count] for i in range(len(lows))]
    rights = refs[1 + total_in : 1 + total_in + count]
    left, right = refs[-5], refs[-4]
    left_sems, right_sems, out_sems = refs[-3:]
    rest = refs[1 + total_in + count : -5]
    outs, stages = rest[: len(rest) // 2], rest[len(rest) // 2 :]
    piece = lefts[0][0].shape[1]
    cols_dev = piece // 64
    width = right.shape[1]
    part_rows = lefts[0][0].shape[0]
    rows = part_rows // 2

    def left_copy(i, q):
        at = slice(i * rows, (i + 1) * rows)
        come = slice(i % 2 * rows, (i % 2 + 1) * rows)
        return pltpu.make_async_copy(
            lefts[i // 2][q].at[come],
            left.at[at, q * piece : (q + 1) * piece],
            left_sems.at[i, q],
        )

    for q in range(count):
        left_copy(0, q).start()
    for q in range(count):
        y = q % planes_y
        begin = 0 if y else start

        def fetch(w, carry):
            n = q * cols_dev + w
            code = table[n]
            shift = lax.shift_right_logical(code, SHIFT)
            at = pl.ds(pl.multiple_of(lax.bitwise_and(code, (1 << SHIFT) - 1), 64), 64)
            for o in range(grid):
                @pl.when(shift == o)
                def _():
                    pltpu.make_async_copy(
                        rights[o * planes_y + y].at[at, begin : begin + width],
                        right.at[pl.ds(pl.multiple_of(n * 64, 64), 64)],
                        right_sems.at[n],
                    ).start()
            return carry

        lax.fori_loop(0, cols_dev, fetch, 0)
    for i in range(1, 2 * len(lows)):
        for q in range(count):
            left_copy(i, q).start()

    def settle(n, carry):
        pltpu.make_async_copy(
            rights[0].at[0:64, 0:width],
            right.at[pl.ds(pl.multiple_of(n * 64, 64), 64)],
            right_sems.at[n],
        ).wait()
        return carry

    lax.fori_loop(0, count * cols_dev, settle, 0)
    sent = []

    def send(n, at):
        sent.append(pltpu.make_async_copy(stages[n].at[at], outs[n].at[at], out_sems.at[len(sent)]))
        sent[-1].start()

    first = 0
    for i in range(2 * len(lows)):
        g = lows[i // 2] + i % 2
        for q in range(count):
            left_copy(i, q).wait()
        block = slice(i * rows, (i + 1) * rows)
        same = slice(i % 2 * rows, (i % 2 + 1) * rows)

        def product(cols):
            return jnp.dot(left[block, :], right[:, cols], preferred_element_type=jnp.float32)

        if g < 2 and direct:
            tiled(width, lambda cols: put_code(stages[first + g], 0, cols, product(cols)))
            send(first + g, slice(0, rows + PAD))
        elif g < 2:
            at = g * (rows + PAD)

            def pair(cols):
                total = product(cols)
                stages[first + 1][same, cols] = total
                put_code(stages[first], at, cols, total)

            tiled(width, pair)
            send(first, slice(at, at + rows + PAD))
            send(first + 1, same)
        elif g == 2:
            tiled(width, lambda cols: put_code(stages[-2], 0, cols, product(cols)))
            send(len(outs) - 2, slice(0, rows + PAD))
        else:

            def own(cols):
                stages[-1][:, cols] = product(cols)

            tiled(width, own)
            send(len(outs) - 1, slice(0, rows))
    for copy in sent:
        copy.wait()


def multiply(table, lefts, rights, lows, direct, grid, planes_y, start, width):
    part_rows, piece = lefts[0][0].shape
    rows = part_rows // 2
    inner = piece * len(lefts[0])
    all_rows = part_rows * len(lows)
    code = jax.ShapeDtypeStruct((rows + PAD, width), jnp.int16)
    outs = []
    if 0 in lows and direct:
        outs += [code, code]
    elif 0 in lows:
        outs += [
            jax.ShapeDtypeStruct((2 * (rows + PAD), width), jnp.int16),
            jax.ShapeDtypeStruct((2 * rows, width), jnp.float32),
        ]
    if 2 in lows:
        outs += [code, jax.ShapeDtypeStruct((rows, width), jnp.float32)]
    hbm = pl.BlockSpec(memory_space=pl.ANY)
    arrays = [v for part in lefts for v in part] + list(rights)
    return pl.pallas_call(
        functools.partial(multiply_kernel, grid, planes_y, lows, direct, start),
        out_shape=outs,
        in_specs=[pl.BlockSpec(memory_space=pltpu.SMEM)] + [hbm] * len(arrays),
        out_specs=[hbm] * len(outs),
        scratch_shapes=[pltpu.VMEM(o.shape, o.dtype) for o in outs]
        + [
            pltpu.VMEM((all_rows, inner), jnp.bfloat16),
            pltpu.VMEM((inner, width), jnp.bfloat16),
            pltpu.SemaphoreType.DMA((2 * len(lows), len(lefts[0]))),
            pltpu.SemaphoreType.DMA((inner // 64,)),
            pltpu.SemaphoreType.DMA((6,)),
        ],
        cost_estimate=pl.CostEstimate(
            flops=2 * all_rows * inner * width,
            transcendentals=0,
            bytes_accessed=2 * inner * (all_rows + width) + 6 * all_rows * width,
        ),
        name="multiply",
    )(table, *arrays)


def relay_kernel(own, code, three, two):
    rows = three.shape[0] - PAD

    def run(cols):
        total = own[0:rows, cols] + decode(code, rows + PAD, cols, rows)
        put_code(three, 0, cols, total)
        total = own[rows : 2 * rows, cols] + decode(code, 0, cols, rows)
        put_code(two, 0, cols, total)

    tiled(own.shape[1], run)


def relay(own, code):
    vmem = pl.BlockSpec(memory_space=pltpu.VMEM)
    out = jax.ShapeDtypeStruct((code.shape[0] // 2, code.shape[1]), code.dtype)
    return pl.pallas_call(
        relay_kernel,
        out_shape=[out, out],
        in_specs=[vmem, vmem],
        out_specs=[vmem, vmem],
        cost_estimate=pl.CostEstimate(
            flops=0, transcendentals=0, bytes_accessed=8 * own.size
        ),
        name="relay",
    )(own, code)


def finish_kernel(start, own, *refs):
    codes, out, stage, sem = refs[:3], refs[-3], refs[-2], refs[-1]
    rows, width = own.shape

    def run(cols):
        total = own[:, cols]
        for code in codes:
            total = total + decode(code, 0, cols, rows)
        stage[:, cols] = total.astype(jnp.bfloat16)

    tiled(width, run)
    copy = pltpu.make_async_copy(stage, out.at[:, start : start + width], sem)
    copy.start()
    copy.wait()


def finish(own, codes, start, full, so_far):
    vmem = pl.BlockSpec(memory_space=pltpu.VMEM)
    hbm = pl.BlockSpec(memory_space=pl.ANY)
    operands = [own, *codes]
    specs = [vmem] * len(operands)
    aliases = {}
    if so_far is not None:
        aliases = {len(operands): 0}
        operands.append(so_far)
        specs.append(hbm)
    return pl.pallas_call(
        functools.partial(finish_kernel, start),
        out_shape=jax.ShapeDtypeStruct((own.shape[0], full), jnp.bfloat16),
        in_specs=specs,
        out_specs=hbm,
        scratch_shapes=[pltpu.VMEM(own.shape, jnp.bfloat16), pltpu.SemaphoreType.DMA(())],
        input_output_aliases=aliases,
        cost_estimate=pl.CostEstimate(
            flops=0, transcendentals=0, bytes_accessed=12 * own.size
        ),
        name="finish",
    )(*operands)


def body(a_blocks, a_mask, a_row_ids, a_col_ids, b_matrix, b_mask):
    grid = lax.axis_size("row")
    depth = lax.axis_size("depth")
    planes_y = depth // LINE
    rows_dev, cols_dev = a_blocks.shape[:2]
    home_rows = rows_dev // depth
    full = b_matrix.shape[1]
    unit = full // sum(CHUNKS)
    widths = [unit * c for c in CHUNKS]
    starts = [sum(widths[:j]) for j in range(len(widths))]

    my_row, my_col = lax.axis_index("row"), lax.axis_index("col")
    my_depth = lax.axis_index("depth")
    my_line, my_near = my_depth // planes_y, my_depth % planes_y
    slots = jnp.arange(4, dtype=jnp.int32)
    meta = jnp.where(
        slots < 2,
        jnp.where(slots == 0, my_row, my_col),
        jnp.where(slots == 2, my_line, my_near),
    )
    stored = jnp.arange(a_row_ids.shape[0], dtype=jnp.int32)
    inverse = jnp.sum(
        jnp.where(a_row_ids[None, :] == stored[:, None], stored[None, :], 0), axis=1
    )
    n = jnp.arange(grid * planes_y * cols_dev, dtype=jnp.int32)
    piece = n // cols_dev
    holder = (my_col + piece // planes_y) % grid * depth
    holder = holder + my_line * planes_y + (my_near + piece % planes_y) % planes_y
    column = holder * cols_dev + n % cols_dev
    every = jnp.arange(a_col_ids.shape[0], dtype=jnp.int32)
    k = jnp.sum(jnp.where(every[None, :] == column[:, None], a_col_ids[None, :], 0), axis=1)
    shift = (k // (cols_dev * depth) - my_row + grid) % grid
    table = shift * (1 << SHIFT) + k % cols_dev * 64
    to = lax.broadcasted_iota(jnp.int32, (cols_dev * 64, cols_dev * 32), 0)
    come = lax.broadcasted_iota(jnp.int32, (cols_dev * 64, cols_dev * 32), 1)
    choose = (come == to % 64 // 2 * cols_dev + to // 64).astype(jnp.bfloat16)

    raws = [a_blocks] + [shifted(a_blocks, "row", o) for o in range(1, grid)]
    masks = [a_mask] + [shifted(a_mask, "row", o) for o in range(1, grid)]
    early = cut(b_matrix, b_mask, widths[:1], 0, False)
    *later, whole = cut(b_matrix, b_mask, widths[1:], widths[0], True)
    cuts = [*early, *later]
    wholes = [whole] + [shifted(whole, "row", o) for o in range(1, grid)]

    parts = []
    for n, low in enumerate((0, 2)):
        near = pick(meta, inverse, masks, choose, raws, (low, low + 1), home_rows, planes_y)
        near = [member(v, planes_y, s) if s else v for s, v in enumerate(near)]
        far = []
        for x in range(1, grid):
            for v in near:
                far.append(shifted(v, "col", x))
        parts.append(near + far)

    product = None
    for j, (start, width, mine) in enumerate(zip(starts, widths, cuts)):
        direct = j >= len(widths) - DIRECT
        near = [member(mine, planes_y, s) for s in range(1, planes_y)]
        rights = [wholes[0]] + near
        for o in range(1, grid):
            rights += [wholes[o]] + [shifted(v, "row", o) for v in near]
        got = []
        for n, lows in enumerate(((0,), (2,)) if j < SPLIT else ((0, 2),)):
            got += multiply(
                table,
                [parts[low // 2] for low in lows],
                rights,
                lows,
                direct,
                grid,
                planes_y,
                start,
                width,
            )
        first, second, beside, own = got
        if direct:
            codes = [hop(first, planes_y, ALL, 3), hop(second, planes_y, ALL, 2)]
        else:
            came = hop(first, planes_y, EDGES, 1)
            three, two = relay(second, came)
            codes = [hop(three, planes_y, INNER, 3), hop(two, planes_y, INNER, 2)]
        codes.append(hop(beside, planes_y, ALL, 1))
        product = finish(own, codes, start, full, product)
    return product


def solution(mesh):
    return jax.shard_map(
        body,
        mesh=mesh,
        in_specs=(
            P("row", ("col", "depth"), None),
            P("row", ("col", "depth")),
            P(),
            P(),
            P(("row", "depth"), "col"),
            P(("row", "depth"), "col"),
        ),
        out_specs=P(("row", "depth"), "col"),
        check_vma=False,
    )
```

```python
import functools
import math

import jax
import jax.numpy as jnp
from jax import lax
from jax.experimental import pallas as pl
from jax.experimental.pallas import tpu as pltpu
from jax.sharding import PartitionSpec as P


LINE = 4
CHUNKS = (2, 3, 5, 2)
SPLIT = 2
DIRECT = 1
SPAN = 32760.0
PAD = 16
SHIFT = 16


def shifted(value, axis, offset):
    size = lax.axis_size(axis)
    return lax.ppermute(value, axis, [((i + offset) % size, i) for i in range(size)])


def member(value, near, offset):
    planes = lax.axis_size("depth") // near
    pairs = [
        (z * near + (y + offset) % near, z * near + y) for z in range(planes) for y in range(near)
    ]
    return lax.ppermute(value, "depth", pairs)


def hop(value, near, senders, flip):
    pairs = [(z * near + y, (z ^ flip) * near + y) for z in senders for y in range(near)]
    return lax.ppermute(value, "depth", pairs)


ALL = tuple(range(LINE))
EDGES = (0, LINE - 1)
INNER = tuple(range(1, LINE - 1))


def encode(total):
    peak = jnp.max(jnp.abs(total), axis=0, keepdims=True)
    level = jnp.ceil(jnp.log2(jnp.maximum(peak, 1e-30)) * 16.0)
    scaled = total * (jnp.exp2(level * (-1.0 / 16.0)) * SPAN)
    return jnp.round(scaled).astype(jnp.int32).astype(jnp.int16), level


def put_code(ref, at, cols, total):
    code, level = encode(total)
    rows = total.shape[0]
    ref[at : at + rows, cols] = code
    ref[at + rows : at + rows + PAD, cols] = (
        jnp.broadcast_to(level, (PAD, level.shape[1])).astype(jnp.int32).astype(jnp.int16)
    )


def decode(ref, at, cols, rows):
    level = ref[at + rows : at + rows + PAD, cols].astype(jnp.int32).astype(jnp.float32)[0:1]
    return ref[at : at + rows, cols].astype(jnp.int32).astype(jnp.float32) * (
        jnp.exp2(level * (1.0 / 16.0)) * (1.0 / SPAN)
    )


def tiled(width, fn):
    step = 256 if width % 256 == 0 else 128

    def run(n, carry):
        fn(pl.ds(pl.multiple_of(n * step, step), step))
        return carry

    lax.fori_loop(0, width // step, run, 0)


def pick_kernel(grid, groups, home_rows, planes_y, *refs):
    meta, inverse = refs[0], refs[1]
    masks = refs[2 : 2 + grid]
    choose = refs[2 + grid]
    raws = refs[3 + grid : 3 + 2 * grid]
    outs = refs[3 + 2 * grid : -2]
    held, sems = refs[-2:]
    rows_dev, cols_dev = raws[0].shape[0], raws[0].shape[1]
    my_row, my_line, my_near = meta[0], meta[2], meta[3]
    depth = LINE * planes_y
    count = len(groups) * home_rows
    batch = math.gcd(count, 4)

    def place(s, t):
        near = lax.rem(my_near - s + planes_y, planes_y)
        g = groups[0] + t // home_rows
        line = lax.bitwise_xor(my_line, LINE - 1 - g)
        block = (my_row * depth + line * planes_y + near) * home_rows + lax.rem(t, home_rows)
        slot = inverse[block]
        owner = lax.rem(lax.div(slot, rows_dev) - my_row + grid, grid)
        return owner, lax.rem(slot, rows_dev)

    def fetch(s):
        def run(t, carry):
            owner, slot = place(s, t)
            for o in range(grid):
                @pl.when(owner == o)
                def _():
                    n = s * count + t
                    pltpu.make_async_copy(raws[o].at[slot], held.at[n], sems.at[n]).start()
            return carry

        lax.fori_loop(0, count, run, 0)

    order = [*range(1, planes_y), 0]
    for s in order:
        fetch(s)
    low = lax.broadcasted_iota(jnp.int32, (64, 128), 1) < 64
    even = lax.broadcasted_iota(jnp.int32, (64, 128), 0) % 2 == 0
    same = low == even
    low_row = lax.broadcasted_iota(jnp.int32, (1, 128), 1) < 64

    def lay(s):
        def run(m, carry):
            stored = []
            for h in range(batch):
                n = s * count + m * batch + h
                pltpu.make_async_copy(raws[0].at[0], held.at[n], sems.at[n]).wait()
                x = held[n].astype(jnp.float32)
                parts = [x[:, 128 * i : 128 * (i + 1)] for i in range(32)]
                stored.append(jnp.concatenate(parts, axis=0).astype(jnp.bfloat16))
            spread = jnp.dot(
                choose[...],
                jnp.concatenate(stored, axis=1),
                preferred_element_type=jnp.float32,
            )
            for h in range(batch):
                t = m * batch + h
                owner, slot = place(s, t)
                for p in range(cols_dev // 2):
                    keep = []
                    for w in (2 * p, 2 * p + 1):
                        flag = masks[0][slot, w]
                        for o in range(1, grid):
                            flag = jnp.where(owner == o, masks[o][slot, w], flag)
                        keep.append(flag)
                    live = jnp.where(low_row, keep[0], keep[1]).astype(jnp.float32)
                    lanes = slice(128 * h, 128 * (h + 1))
                    first = spread[2 * p * 64 : (2 * p + 1) * 64, lanes]
                    second = spread[(2 * p + 1) * 64 : (2 * p + 2) * 64, lanes]
                    straight = jnp.where(low, first, second)
                    turned = pltpu.roll(jnp.where(low, second, first), 64, 1)
                    pair = jnp.where(same, straight, turned) * live
                    at = pl.ds(pl.multiple_of(t * 64, 64), 64)
                    outs[s][at, p * 128 : (p + 1) * 128] = pair.astype(jnp.bfloat16)
            return carry

        lax.fori_loop(0, count // batch, run, 0)

    for s in order:
        lay(s)


def pick(meta, inverse, masks, choose, raws, groups, home_rows, planes_y):
    grid = len(raws)
    cols_dev, side2 = raws[0].shape[1:]
    count = len(groups) * home_rows
    total = count * planes_y
    smem = pl.BlockSpec(memory_space=pltpu.SMEM)
    vmem = pl.BlockSpec(memory_space=pltpu.VMEM)
    shape = jax.ShapeDtypeStruct((count * 64, cols_dev * 64), jnp.bfloat16)
    return pl.pallas_call(
        functools.partial(pick_kernel, grid, groups, home_rows, planes_y),
        out_shape=[shape] * planes_y,
        in_specs=[smem] * (2 + grid) + [vmem] + [pl.BlockSpec(memory_space=pl.ANY)] * grid,
        out_specs=[vmem] * planes_y,
        scratch_shapes=[
            pltpu.VMEM((total, cols_dev, side2), jnp.bfloat16),
            pltpu.SemaphoreType.DMA((total,)),
        ],
        cost_estimate=pl.CostEstimate(
            flops=0, transcendentals=0, bytes_accessed=4 * total * cols_dev * side2
        ),
        name="pick",
    )(meta, inverse, *masks, choose, *raws)


def cut_kernel(widths, begin, wide, mask, b, *outs):
    blocks = mask.shape[0]
    shape = (mask.shape[1], b.shape[1])
    expand = (
        lax.broadcasted_iota(jnp.int32, shape, 1) // 64
        == lax.broadcasted_iota(jnp.int32, shape, 0)
    ).astype(jnp.float32)
    live = jnp.dot(
        mask[...].astype(jnp.float32), expand, preferred_element_type=jnp.float32
    ).astype(jnp.bfloat16)
    spans = [(sum(widths[:i]) + begin, w, outs[i]) for i, w in enumerate(widths)]
    if wide:
        spans = [(0, begin, None)] + spans
    for s in range(blocks):
        rows = slice(s * 64, (s + 1) * 64)
        for start, width, out in spans:
            cols = slice(start, start + width)
            kept = b[rows, cols] * live[s : s + 1, cols]
            if out is not None:
                out[rows, :] = kept
            if wide:
                outs[-1][rows, cols] = kept


def cut(b_matrix, b_mask, widths, begin, wide):
    vmem = pl.BlockSpec(memory_space=pltpu.VMEM)
    rows, full = b_matrix.shape
    read = full if wide else begin + sum(widths)
    outs = [*widths, full] if wide else widths

    def whole(shape):
        return pl.BlockSpec(shape, lambda i: (0, 0))

    return pl.pallas_call(
        functools.partial(cut_kernel, widths, begin, wide),
        grid=(1,),
        out_shape=[jax.ShapeDtypeStruct((rows, w), jnp.bfloat16) for w in outs],
        in_specs=[whole(b_mask.shape), whole((rows, read))],
        out_specs=[whole((rows, w)) for w in outs],
        cost_estimate=pl.CostEstimate(
            flops=0, transcendentals=0, bytes_accessed=6 * rows * read
        ),
        name="cut",
    )(b_mask, b_matrix)


def multiply_kernel(grid, planes_y, lows, direct, start, *refs):
    table = refs[0]
    count = grid * planes_y
    total_in = count * len(lows)
    lefts = [refs[1 + i * count : 1 + (i + 1) * count] for i in range(len(lows))]
    rights = refs[1 + total_in : 1 + total_in + count]
    left, right = refs[-5], refs[-4]
    left_sems, right_sems, out_sems = refs[-3:]
    rest = refs[1 + total_in + count : -5]
    outs, stages = rest[: len(rest) // 2], rest[len(rest) // 2 :]
    piece = lefts[0][0].shape[1]
    cols_dev = piece // 64
    width = right.shape[1]
    part_rows = lefts[0][0].shape[0]
    rows = part_rows // 2

    def left_copy(i, q):
        at = slice(i * rows, (i + 1) * rows)
        come = slice(i % 2 * rows, (i % 2 + 1) * rows)
        return pltpu.make_async_copy(
            lefts[i // 2][q].at[come],
            left.at[at, q * piece : (q + 1) * piece],
            left_sems.at[i, q],
        )

    for q in range(count):
        left_copy(0, q).start()
    for q in range(count):
        y = q % planes_y
        begin = 0 if y else start

        for w in range(cols_dev):
            n = q * cols_dev + w
            code = table[n]
            at = pl.ds(pl.multiple_of(lax.bitwise_and(code, (1 << SHIFT) - 1), 64), 64)
            for o in range(grid):
                @pl.when(lax.shift_right_logical(code, SHIFT) == o)
                def _():
                    pltpu.make_async_copy(
                        rights[o * planes_y + y].at[at, begin : begin + width],
                        right.at[n * 64 : (n + 1) * 64],
                        right_sems.at[n],
                    ).start()
    for i in range(1, 2 * len(lows)):
        for q in range(count):
            left_copy(i, q).start()

    for n in range(count * cols_dev):
        pltpu.make_async_copy(
            rights[0].at[0:64, 0:width], right.at[n * 64 : (n + 1) * 64], right_sems.at[n]
        ).wait()
    sent = []

    def send(n, at):
        sent.append(pltpu.make_async_copy(stages[n].at[at], outs[n].at[at], out_sems.at[len(sent)]))
        sent[-1].start()

    first = 0
    for i in range(2 * len(lows)):
        g = lows[i // 2] + i % 2
        for q in range(count):
            left_copy(i, q).wait()
        block = slice(i * rows, (i + 1) * rows)
        same = slice(i % 2 * rows, (i % 2 + 1) * rows)

        def product(cols):
            return jnp.dot(left[block, :], right[:, cols], preferred_element_type=jnp.float32)

        if g < 2 and direct:
            tiled(width, lambda cols: put_code(stages[first + g], 0, cols, product(cols)))
            send(first + g, slice(0, rows + PAD))
        elif g < 2:
            at = g * (rows + PAD)

            def pair(cols):
                total = product(cols)
                stages[first + 1][same, cols] = total
                put_code(stages[first], at, cols, total)

            tiled(width, pair)
            send(first, slice(at, at + rows + PAD))
            send(first + 1, same)
        elif g == 2:
            tiled(width, lambda cols: put_code(stages[-2], 0, cols, product(cols)))
            send(len(outs) - 2, slice(0, rows + PAD))
        else:

            def own(cols):
                stages[-1][:, cols] = product(cols)

            tiled(width, own)
            send(len(outs) - 1, slice(0, rows))
    for copy in sent:
        copy.wait()


def multiply(table, lefts, rights, lows, direct, grid, planes_y, start, width):
    part_rows, piece = lefts[0][0].shape
    rows = part_rows // 2
    inner = piece * len(lefts[0])
    all_rows = part_rows * len(lows)
    code = jax.ShapeDtypeStruct((rows + PAD, width), jnp.int16)
    outs = []
    if 0 in lows and direct:
        outs += [code, code]
    elif 0 in lows:
        outs += [
            jax.ShapeDtypeStruct((2 * (rows + PAD), width), jnp.int16),
            jax.ShapeDtypeStruct((2 * rows, width), jnp.float32),
        ]
    if 2 in lows:
        outs += [code, jax.ShapeDtypeStruct((rows, width), jnp.float32)]
    hbm = pl.BlockSpec(memory_space=pl.ANY)
    arrays = [v for part in lefts for v in part] + list(rights)
    return pl.pallas_call(
        functools.partial(multiply_kernel, grid, planes_y, lows, direct, start),
        out_shape=outs,
        in_specs=[pl.BlockSpec(memory_space=pltpu.SMEM)] + [hbm] * len(arrays),
        out_specs=[hbm] * len(outs),
        scratch_shapes=[pltpu.VMEM(o.shape, o.dtype) for o in outs]
        + [
            pltpu.VMEM((all_rows, inner), jnp.bfloat16),
            pltpu.VMEM((inner, width), jnp.bfloat16),
            pltpu.SemaphoreType.DMA((2 * len(lows), len(lefts[0]))),
            pltpu.SemaphoreType.DMA((inner // 64,)),
            pltpu.SemaphoreType.DMA((6,)),
        ],
        cost_estimate=pl.CostEstimate(
            flops=2 * all_rows * inner * width,
            transcendentals=0,
            bytes_accessed=2 * inner * (all_rows + width) + 6 * all_rows * width,
        ),
        name="multiply",
    )(table, *arrays)


def relay_kernel(own, code, three, two):
    rows = three.shape[0] - PAD

    def run(cols):
        total = own[0:rows, cols] + decode(code, rows + PAD, cols, rows)
        put_code(three, 0, cols, total)
        total = own[rows : 2 * rows, cols] + decode(code, 0, cols, rows)
        put_code(two, 0, cols, total)

    tiled(own.shape[1], run)


def relay(own, code):
    vmem = pl.BlockSpec(memory_space=pltpu.VMEM)
    out = jax.ShapeDtypeStruct((code.shape[0] // 2, code.shape[1]), code.dtype)
    return pl.pallas_call(
        relay_kernel,
        out_shape=[out, out],
        in_specs=[vmem, vmem],
        out_specs=[vmem, vmem],
        cost_estimate=pl.CostEstimate(
            flops=0, transcendentals=0, bytes_accessed=8 * own.size
        ),
        name="relay",
    )(own, code)


def finish_kernel(start, own, *refs):
    codes, out, stage, sem = refs[:3], refs[-3], refs[-2], refs[-1]
    rows, width = own.shape

    def run(cols):
        total = own[:, cols]
        for code in codes:
            total = total + decode(code, 0, cols, rows)
        stage[:, cols] = total.astype(jnp.bfloat16)

    tiled(width, run)
    copy = pltpu.make_async_copy(stage, out.at[:, start : start + width], sem)
    copy.start()
    copy.wait()


def finish(own, codes, start, full, so_far):
    vmem = pl.BlockSpec(memory_space=pltpu.VMEM)
    hbm = pl.BlockSpec(memory_space=pl.ANY)
    operands = [own, *codes]
    specs = [vmem] * len(operands)
    aliases = {}
    if so_far is not None:
        aliases = {len(operands): 0}
        operands.append(so_far)
        specs.append(hbm)
    return pl.pallas_call(
        functools.partial(finish_kernel, start),
        out_shape=jax.ShapeDtypeStruct((own.shape[0], full), jnp.bfloat16),
        in_specs=specs,
        out_specs=hbm,
        scratch_shapes=[pltpu.VMEM(own.shape, jnp.bfloat16), pltpu.SemaphoreType.DMA(())],
        input_output_aliases=aliases,
        cost_estimate=pl.CostEstimate(
            flops=0, transcendentals=0, bytes_accessed=12 * own.size
        ),
        name="finish",
    )(*operands)


def body(a_blocks, a_mask, a_row_ids, a_col_ids, b_matrix, b_mask):
    grid = lax.axis_size("row")
    depth = lax.axis_size("depth")
    planes_y = depth // LINE
    rows_dev, cols_dev = a_blocks.shape[:2]
    home_rows = rows_dev // depth
    full = b_matrix.shape[1]
    unit = full // sum(CHUNKS)
    widths = [unit * c for c in CHUNKS]
    starts = [sum(widths[:j]) for j in range(len(widths))]

    my_row, my_col = lax.axis_index("row"), lax.axis_index("col")
    my_depth = lax.axis_index("depth")
    my_line, my_near = my_depth // planes_y, my_depth % planes_y
    slots = jnp.arange(4, dtype=jnp.int32)
    meta = jnp.where(
        slots < 2,
        jnp.where(slots == 0, my_row, my_col),
        jnp.where(slots == 2, my_line, my_near),
    )
    stored = jnp.arange(a_row_ids.shape[0], dtype=jnp.int32)
    inverse = jnp.sum(
        jnp.where(a_row_ids[None, :] == stored[:, None], stored[None, :], 0), axis=1
    )
    n = jnp.arange(grid * planes_y * cols_dev, dtype=jnp.int32)
    piece = n // cols_dev
    holder = (my_col + piece // planes_y) % grid * depth
    holder = holder + my_line * planes_y + (my_near + piece % planes_y) % planes_y
    column = holder * cols_dev + n % cols_dev
    every = jnp.arange(a_col_ids.shape[0], dtype=jnp.int32)
    k = jnp.sum(jnp.where(every[None, :] == column[:, None], a_col_ids[None, :], 0), axis=1)
    shift = (k // (cols_dev * depth) - my_row + grid) % grid
    table = shift * (1 << SHIFT) + k % cols_dev * 64
    to = lax.broadcasted_iota(jnp.int32, (cols_dev * 64, cols_dev * 32), 0)
    come = lax.broadcasted_iota(jnp.int32, (cols_dev * 64, cols_dev * 32), 1)
    choose = (come == to % 64 // 2 * cols_dev + to // 64).astype(jnp.bfloat16)

    raws = [a_blocks] + [shifted(a_blocks, "row", o) for o in range(1, grid)]
    masks = [a_mask] + [shifted(a_mask, "row", o) for o in range(1, grid)]
    early = cut(b_matrix, b_mask, widths[:1], 0, False)
    *later, whole = cut(b_matrix, b_mask, widths[1:], widths[0], True)
    cuts = [*early, *later]
    wholes = [whole] + [shifted(whole, "row", o) for o in range(1, grid)]

    parts = []
    for n, low in enumerate((0, 2)):
        near = pick(meta, inverse, masks, choose, raws, (low, low + 1), home_rows, planes_y)
        near = [member(v, planes_y, s) if s else v for s, v in enumerate(near)]
        far = []
        for x in range(1, grid):
            for v in near:
                far.append(shifted(v, "col", x))
        parts.append(near + far)

    product = None
    for j, (start, width, mine) in enumerate(zip(starts, widths, cuts)):
        direct = j >= len(widths) - DIRECT
        near = [member(mine, planes_y, s) for s in range(1, planes_y)]
        rights = [wholes[0]] + near
        for o in range(1, grid):
            rights += [wholes[o]] + [shifted(v, "row", o) for v in near]
        got = []
        for n, lows in enumerate(((0,), (2,)) if j < SPLIT else ((0, 2),)):
            got += multiply(
                table,
                [parts[low // 2] for low in lows],
                rights,
                lows,
                direct,
                grid,
                planes_y,
                start,
                width,
            )
        first, second, beside, own = got
        if direct:
            codes = [hop(first, planes_y, ALL, 3), hop(second, planes_y, ALL, 2)]
        else:
            came = hop(first, planes_y, EDGES, 1)
            three, two = relay(second, came)
            codes = [hop(three, planes_y, INNER, 3), hop(two, planes_y, INNER, 2)]
        codes.append(hop(beside, planes_y, ALL, 1))
        product = finish(own, codes, start, full, product)
    return product


def solution(mesh):
    return jax.shard_map(
        body,
        mesh=mesh,
        in_specs=(
            P("row", ("col", "depth"), None),
            P("row", ("col", "depth")),
            P(),
            P(),
            P(("row", "depth"), "col"),
            P(("row", "depth"), "col"),
        ),
        out_specs=P(("row", "depth"), "col"),
        check_vma=False,
    )
```

```python
import functools
import math

import jax
import jax.numpy as jnp
from jax import lax
from jax.experimental import pallas as pl
from jax.experimental.pallas import tpu as pltpu
from jax.sharding import PartitionSpec as P


LINE = 4
CHUNKS = (2, 3, 3, 2, 2)
SPLIT = 3
DIRECT = 1
SPAN = 32760.0
PAD = 16
SHIFT = 16


def shifted(value, axis, offset):
    size = lax.axis_size(axis)
    return lax.ppermute(value, axis, [((i + offset) % size, i) for i in range(size)])


def member(value, near, offset):
    planes = lax.axis_size("depth") // near
    pairs = [
        (z * near + (y + offset) % near, z * near + y) for z in range(planes) for y in range(near)
    ]
    return lax.ppermute(value, "depth", pairs)


def hop(value, near, senders, flip):
    pairs = [(z * near + y, (z ^ flip) * near + y) for z in senders for y in range(near)]
    return lax.ppermute(value, "depth", pairs)


ALL = tuple(range(LINE))
EDGES = (0, LINE - 1)
INNER = tuple(range(1, LINE - 1))


def encode(total):
    peak = jnp.max(jnp.abs(total), axis=0, keepdims=True)
    level = jnp.ceil(jnp.log2(jnp.maximum(peak, 1e-30)) * 16.0)
    scaled = total * (jnp.exp2(level * (-1.0 / 16.0)) * SPAN)
    return jnp.round(scaled).astype(jnp.int32).astype(jnp.int16), level


def put_code(ref, at, cols, total):
    code, level = encode(total)
    rows = total.shape[0]
    ref[at : at + rows, cols] = code
    ref[at + rows : at + rows + PAD, cols] = (
        jnp.broadcast_to(level, (PAD, level.shape[1])).astype(jnp.int32).astype(jnp.int16)
    )


def decode(ref, at, cols, rows):
    level = ref[at + rows : at + rows + PAD, cols].astype(jnp.int32).astype(jnp.float32)[0:1]
    return ref[at : at + rows, cols].astype(jnp.int32).astype(jnp.float32) * (
        jnp.exp2(level * (1.0 / 16.0)) * (1.0 / SPAN)
    )


def tile_of(width):
    return 256 if width % 256 == 0 else 128


def tiled(width, fn):
    step = tile_of(width)

    def run(n, carry):
        fn(pl.ds(pl.multiple_of(n * step, step), step))
        return carry

    lax.fori_loop(0, width // step, run, 0)


def pick_kernel(grid, groups, home_rows, planes_y, members, *refs):
    meta, inverse = refs[0], refs[1]
    masks = refs[2 : 2 + grid]
    choose = refs[2 + grid]
    raws = refs[3 + grid : 3 + 2 * grid]
    outs = refs[3 + 2 * grid : -2]
    held, sems = refs[-2:]
    rows_dev, cols_dev = raws[0].shape[0], raws[0].shape[1]
    my_row, my_line, my_near = meta[0], meta[2], meta[3]
    depth = LINE * planes_y
    count = len(groups) * home_rows
    batch = math.gcd(count, 4)

    def place(s, t):
        near = lax.rem(my_near - s + planes_y, planes_y)
        g = groups[0] + t // home_rows
        line = lax.bitwise_xor(my_line, LINE - 1 - g)
        block = (my_row * depth + line * planes_y + near) * home_rows + lax.rem(t, home_rows)
        slot = inverse[block]
        owner = lax.rem(lax.div(slot, rows_dev) - my_row + grid, grid)
        return owner, lax.rem(slot, rows_dev)

    def fetch(s):
        def run(t, carry):
            owner, slot = place(s, t)
            for o in range(grid):
                @pl.when(owner == o)
                def _():
                    n = members.index(s) * count + t
                    pltpu.make_async_copy(raws[o].at[slot], held.at[n], sems.at[n]).start()
            return carry

        lax.fori_loop(0, count, run, 0)

    for s in members:
        fetch(s)
    low = lax.broadcasted_iota(jnp.int32, (64, 128), 1) < 64
    even = lax.broadcasted_iota(jnp.int32, (64, 128), 0) % 2 == 0
    same = low == even
    low_row = lax.broadcasted_iota(jnp.int32, (1, 128), 1) < 64

    def lay(s):
        def run(m, carry):
            stored = []
            for h in range(batch):
                n = members.index(s) * count + m * batch + h
                pltpu.make_async_copy(raws[0].at[0], held.at[n], sems.at[n]).wait()
                x = held[n].astype(jnp.float32)
                parts = [x[:, 128 * i : 128 * (i + 1)] for i in range(32)]
                stored.append(jnp.concatenate(parts, axis=0).astype(jnp.bfloat16))
            spread = jnp.dot(
                choose[...],
                jnp.concatenate(stored, axis=1),
                preferred_element_type=jnp.float32,
            )
            for h in range(batch):
                t = m * batch + h
                owner, slot = place(s, t)
                for p in range(cols_dev // 2):
                    keep = []
                    for w in (2 * p, 2 * p + 1):
                        flag = masks[0][slot, w]
                        for o in range(1, grid):
                            flag = jnp.where(owner == o, masks[o][slot, w], flag)
                        keep.append(flag)
                    live = jnp.where(low_row, keep[0], keep[1]).astype(jnp.float32)
                    lanes = slice(128 * h, 128 * (h + 1))
                    first = spread[2 * p * 64 : (2 * p + 1) * 64, lanes]
                    second = spread[(2 * p + 1) * 64 : (2 * p + 2) * 64, lanes]
                    straight = jnp.where(low, first, second)
                    turned = pltpu.roll(jnp.where(low, second, first), 64, 1)
                    pair = jnp.where(same, straight, turned) * live
                    at = pl.ds(pl.multiple_of(t * 64, 64), 64)
                    outs[members.index(s)][at, p * 128 : (p + 1) * 128] = pair.astype(jnp.bfloat16)
            return carry

        lax.fori_loop(0, count // batch, run, 0)

    for s in members:
        lay(s)


def pick(meta, inverse, masks, choose, raws, groups, home_rows, planes_y, members):
    grid = len(raws)
    cols_dev, side2 = raws[0].shape[1:]
    count = len(groups) * home_rows
    total = count * len(members)
    smem = pl.BlockSpec(memory_space=pltpu.SMEM)
    vmem = pl.BlockSpec(memory_space=pltpu.VMEM)
    shape = jax.ShapeDtypeStruct((count * 64, cols_dev * 64), jnp.bfloat16)
    return pl.pallas_call(
        functools.partial(pick_kernel, grid, groups, home_rows, planes_y, members),
        out_shape=[shape] * len(members),
        in_specs=[smem] * (2 + grid) + [vmem] + [pl.BlockSpec(memory_space=pltpu.HBM)] * grid,
        out_specs=[vmem] * len(members),
        scratch_shapes=[
            pltpu.VMEM((total, cols_dev, side2), jnp.bfloat16),
            pltpu.SemaphoreType.DMA((total,)),
        ],
        cost_estimate=pl.CostEstimate(
            flops=0, transcendentals=0, bytes_accessed=4 * total * cols_dev * side2
        ),
        name="pick",
    )(meta, inverse, *masks, choose, *raws)


def cut_kernel(widths, begin, wide, mask, b, *outs):
    blocks = mask.shape[0]
    shape = (mask.shape[1], b.shape[1])
    expand = (
        lax.broadcasted_iota(jnp.int32, shape, 1) // 64
        == lax.broadcasted_iota(jnp.int32, shape, 0)
    ).astype(jnp.float32)
    live = jnp.dot(
        mask[...].astype(jnp.float32), expand, preferred_element_type=jnp.float32
    ).astype(jnp.bfloat16)
    spans = [(sum(widths[:i]) + begin, w, outs[i]) for i, w in enumerate(widths)]
    if wide:
        spans = [(0, begin, None)] + spans
    for s in range(blocks):
        rows = slice(s * 64, (s + 1) * 64)
        for start, width, out in spans:
            cols = slice(start, start + width)
            kept = b[rows, cols] * live[s : s + 1, cols]
            if out is not None:
                out[rows, :] = kept
            if wide:
                outs[-1][rows, cols] = kept


def cut(b_matrix, b_mask, widths, begin, wide):
    vmem = pl.BlockSpec(memory_space=pltpu.VMEM)
    rows, full = b_matrix.shape
    read = full if wide else begin + sum(widths)
    outs = [*widths, full] if wide else widths

    def whole(shape):
        return pl.BlockSpec(shape, lambda i: (0, 0))

    return pl.pallas_call(
        functools.partial(cut_kernel, widths, begin, wide),
        grid=(1,),
        out_shape=[jax.ShapeDtypeStruct((rows, w), jnp.bfloat16) for w in outs],
        in_specs=[whole(b_mask.shape), whole((rows, read))],
        out_specs=[whole((rows, w)) for w in outs],
        cost_estimate=pl.CostEstimate(
            flops=0, transcendentals=0, bytes_accessed=6 * rows * read
        ),
        name="cut",
    )(b_mask, b_matrix)


def multiply_kernel(grid, planes_y, lows, direct, start, *refs):
    table = refs[0]
    count = grid * planes_y
    total_in = count * len(lows)
    lefts = [refs[1 + i * count : 1 + (i + 1) * count] for i in range(len(lows))]
    rights = refs[1 + total_in : 1 + total_in + count]
    left, right = refs[-5], refs[-4]
    left_sems, right_sems, out_sems = refs[-3:]
    rest = refs[1 + total_in + count : -5]
    outs, stages = rest[: len(rest) // 2], rest[len(rest) // 2 :]
    piece = lefts[0][0].shape[1]
    cols_dev = piece // 64
    width = right.shape[1]
    part_rows = lefts[0][0].shape[0]
    rows = part_rows // 2

    step = tile_of(width)

    def left_fetch(i):
        come = slice(i % 2 * rows, (i % 2 + 1) * rows)
        for q in range(count):
            pltpu.make_async_copy(
                lefts[i // 2][q].at[come],
                left.at[i * rows : (i + 1) * rows, q * piece : (q + 1) * piece],
                left_sems.at[i],
            ).start()

    def left_wait(i):
        held = left.at[i * rows : (i + 1) * rows, :]
        pltpu.make_async_copy(held, held, left_sems.at[i]).wait()

    def right_wait(n):
        held = right.at[:, pl.ds(pl.multiple_of(n * step, step), step)]
        pltpu.make_async_copy(held, held, right_sems.at[n]).wait()

    left_fetch(0)
    for n in range(width // step):
        for q in range(count):
            begin = n * step + (0 if q % planes_y else start)
            for w in range(cols_dev):
                row = q * cols_dev + w
                code = table[row]
                at = pl.ds(pl.multiple_of(lax.bitwise_and(code, (1 << SHIFT) - 1), 64), 64)
                for o in range(grid):
                    @pl.when(lax.shift_right_logical(code, SHIFT) == o)
                    def _():
                        pltpu.make_async_copy(
                            rights[o * planes_y + q % planes_y].at[at, begin : begin + step],
                            right.at[row * 64 : (row + 1) * 64, n * step : (n + 1) * step],
                            right_sems.at[n],
                        ).start()
    for i in range(1, 2 * len(lows)):
        left_fetch(i)
    sent = []

    def send(n, at):
        sent.append(pltpu.make_async_copy(stages[n].at[at], outs[n].at[at], out_sems.at[len(sent)]))
        sent[-1].start()

    first = 0
    for i in range(2 * len(lows)):
        g = lows[i // 2] + i % 2
        left_wait(i)
        block = slice(i * rows, (i + 1) * rows)
        same = slice(i % 2 * rows, (i % 2 + 1) * rows)

        def product(cols):
            if i == 0:
                right_wait(cols.start // step)
            return jnp.dot(left[block, :], right[:, cols], preferred_element_type=jnp.float32)

        if g < 2 and direct:
            tiled(width, lambda cols: put_code(stages[first + g], 0, cols, product(cols)))
            send(first + g, slice(0, rows + PAD))
        elif g < 2:
            at = g * (rows + PAD)

            def pair(cols):
                total = product(cols)
                stages[first + 1][same, cols] = total
                put_code(stages[first], at, cols, total)

            tiled(width, pair)
            send(first, slice(at, at + rows + PAD))
            send(first + 1, same)
        elif g == 2:
            tiled(width, lambda cols: put_code(stages[-2], 0, cols, product(cols)))
            send(len(outs) - 2, slice(0, rows + PAD))
        else:

            def own(cols):
                stages[-1][:, cols] = product(cols)

            tiled(width, own)
            send(len(outs) - 1, slice(0, rows))
    for copy in sent:
        copy.wait()


def multiply(table, lefts, rights, lows, direct, grid, planes_y, start, width):
    part_rows, piece = lefts[0][0].shape
    rows = part_rows // 2
    inner = piece * len(lefts[0])
    all_rows = part_rows * len(lows)
    code = jax.ShapeDtypeStruct((rows + PAD, width), jnp.int16)
    outs = []
    if 0 in lows and direct:
        outs += [code, code]
    elif 0 in lows:
        outs += [
            jax.ShapeDtypeStruct((2 * (rows + PAD), width), jnp.int16),
            jax.ShapeDtypeStruct((2 * rows, width), jnp.float32),
        ]
    if 2 in lows:
        outs += [code, jax.ShapeDtypeStruct((rows, width), jnp.float32)]
    hbm = pl.BlockSpec(memory_space=pltpu.HBM)
    arrays = [v for part in lefts for v in part] + list(rights)
    return pl.pallas_call(
        functools.partial(multiply_kernel, grid, planes_y, lows, direct, start),
        out_shape=outs,
        in_specs=[pl.BlockSpec(memory_space=pltpu.SMEM)] + [hbm] * len(arrays),
        out_specs=[hbm] * len(outs),
        scratch_shapes=[pltpu.VMEM(o.shape, o.dtype) for o in outs]
        + [
            pltpu.VMEM((all_rows, inner), jnp.bfloat16),
            pltpu.VMEM((inner, width), jnp.bfloat16),
            pltpu.SemaphoreType.DMA((2 * len(lows),)),
            pltpu.SemaphoreType.DMA((width // tile_of(width),)),
            pltpu.SemaphoreType.DMA((6,)),
        ],
        cost_estimate=pl.CostEstimate(
            flops=2 * all_rows * inner * width,
            transcendentals=0,
            bytes_accessed=2 * inner * (all_rows + width) + 6 * all_rows * width,
        ),
        name="multiply",
    )(table, *arrays)


def relay_kernel(own, code, three, two):
    rows = three.shape[0] - PAD

    def run(cols):
        total = own[0:rows, cols] + decode(code, rows + PAD, cols, rows)
        put_code(three, 0, cols, total)
        total = own[rows : 2 * rows, cols] + decode(code, 0, cols, rows)
        put_code(two, 0, cols, total)

    tiled(own.shape[1], run)


def relay(own, code):
    vmem = pl.BlockSpec(memory_space=pltpu.VMEM)
    out = jax.ShapeDtypeStruct((code.shape[0] // 2, code.shape[1]), code.dtype)
    return pl.pallas_call(
        relay_kernel,
        out_shape=[out, out],
        in_specs=[vmem, vmem],
        out_specs=[vmem, vmem],
        cost_estimate=pl.CostEstimate(
            flops=0, transcendentals=0, bytes_accessed=8 * own.size
        ),
        name="relay",
    )(own, code)


def finish_kernel(start, own, *refs):
    codes, out, stage, sem = refs[:3], refs[-3], refs[-2], refs[-1]
    rows, width = own.shape

    def run(cols):
        total = own[:, cols]
        for code in codes:
            total = total + decode(code, 0, cols, rows)
        stage[:, cols] = total.astype(jnp.bfloat16)

    tiled(width, run)
    copy = pltpu.make_async_copy(stage, out.at[:, start : start + width], sem)
    copy.start()
    copy.wait()


def finish(own, codes, start, full, so_far):
    vmem = pl.BlockSpec(memory_space=pltpu.VMEM)
    hbm = pl.BlockSpec(memory_space=pltpu.HBM)
    operands = [own, *codes]
    specs = [vmem] * len(operands)
    aliases = {}
    if so_far is not None:
        aliases = {len(operands): 0}
        operands.append(so_far)
        specs.append(hbm)
    return pl.pallas_call(
        functools.partial(finish_kernel, start),
        out_shape=jax.ShapeDtypeStruct((own.shape[0], full), jnp.bfloat16),
        in_specs=specs,
        out_specs=hbm,
        scratch_shapes=[pltpu.VMEM(own.shape, jnp.bfloat16), pltpu.SemaphoreType.DMA(())],
        input_output_aliases=aliases,
        cost_estimate=pl.CostEstimate(
            flops=0, transcendentals=0, bytes_accessed=12 * own.size
        ),
        name="finish",
    )(*operands)


def body(a_blocks, a_mask, a_row_ids, a_col_ids, b_matrix, b_mask):
    grid = lax.axis_size("row")
    depth = lax.axis_size("depth")
    planes_y = depth // LINE
    rows_dev, cols_dev = a_blocks.shape[:2]
    home_rows = rows_dev // depth
    full = b_matrix.shape[1]
    unit = full // sum(CHUNKS)
    widths = [unit * c for c in CHUNKS]
    starts = [sum(widths[:j]) for j in range(len(widths))]

    my_row, my_col = lax.axis_index("row"), lax.axis_index("col")
    my_depth = lax.axis_index("depth")
    my_line, my_near = my_depth // planes_y, my_depth % planes_y
    slots = jnp.arange(4, dtype=jnp.int32)
    meta = jnp.where(
        slots < 2,
        jnp.where(slots == 0, my_row, my_col),
        jnp.where(slots == 2, my_line, my_near),
    )
    stored = jnp.arange(a_row_ids.shape[0], dtype=jnp.int32)
    inverse = jnp.sum(
        jnp.where(a_row_ids[None, :] == stored[:, None], stored[None, :], 0), axis=1
    )
    n = jnp.arange(grid * planes_y * cols_dev, dtype=jnp.int32)
    piece = n // cols_dev
    holder = (my_col + piece // planes_y) % grid * depth
    holder = holder + my_line * planes_y + (my_near + piece % planes_y) % planes_y
    column = holder * cols_dev + n % cols_dev
    every = jnp.arange(a_col_ids.shape[0], dtype=jnp.int32)
    k = jnp.sum(jnp.where(every[None, :] == column[:, None], a_col_ids[None, :], 0), axis=1)
    shift = (k // (cols_dev * depth) - my_row + grid) % grid
    table = shift * (1 << SHIFT) + k % cols_dev * 64
    to = lax.broadcasted_iota(jnp.int32, (cols_dev * 64, cols_dev * 32), 0)
    come = lax.broadcasted_iota(jnp.int32, (cols_dev * 64, cols_dev * 32), 1)
    choose = (come == to % 64 // 2 * cols_dev + to // 64).astype(jnp.bfloat16)

    raws = [a_blocks] + [shifted(a_blocks, "row", o) for o in range(1, grid)]
    masks = [a_mask] + [shifted(a_mask, "row", o) for o in range(1, grid)]
    early = cut(b_matrix, b_mask, widths[:1], 0, False)
    *later, whole = cut(b_matrix, b_mask, widths[1:], widths[0], True)
    cuts = [*early, *later]
    wholes = [whole] + [shifted(whole, "row", o) for o in range(1, grid)]

    parts = []
    for n, low in enumerate((0, 2)):
        near = []
        for members in (range(1, planes_y), range(1)):
            picked = pick(
                meta,
                inverse,
                masks,
                choose,
                raws,
                (low, low + 1),
                home_rows,
                planes_y,
                tuple(members),
            )
            near = list(picked) + near
        near = [member(v, planes_y, s) if s else v for s, v in enumerate(near)]
        far = []
        for x in range(1, grid):
            for v in near:
                far.append(shifted(v, "col", x))
        parts.append(near + far)

    product = None
    for j, (start, width, mine) in enumerate(zip(starts, widths, cuts)):
        direct = j >= len(widths) - DIRECT
        near = [member(mine, planes_y, s) for s in range(1, planes_y)]
        rights = [wholes[0]] + near
        for o in range(1, grid):
            rights += [wholes[o]] + [shifted(v, "row", o) for v in near]
        got = []
        for n, lows in enumerate(((0,), (2,)) if j < SPLIT else ((0, 2),)):
            got += multiply(
                table,
                [parts[low // 2] for low in lows],
                rights,
                lows,
                direct,
                grid,
                planes_y,
                start,
                width,
            )
        first, second, beside, own = got
        if direct:
            codes = [hop(first, planes_y, ALL, 3), hop(second, planes_y, ALL, 2)]
        else:
            came = hop(first, planes_y, EDGES, 1)
            three, two = relay(second, came)
            codes = [hop(three, planes_y, INNER, 3), hop(two, planes_y, INNER, 2)]
        codes.append(hop(beside, planes_y, ALL, 1))
        product = finish(own, codes, start, full, product)
    return product


def solution(mesh):
    return jax.shard_map(
        body,
        mesh=mesh,
        in_specs=(
            P("row", ("col", "depth"), None),
            P("row", ("col", "depth")),
            P(),
            P(),
            P(("row", "depth"), "col"),
            P(("row", "depth"), "col"),
        ),
        out_specs=P(("row", "depth"), "col"),
        check_vma=False,
    )
```

```python
import functools
import math

import jax
import jax.numpy as jnp
from jax import lax
from jax.experimental import pallas as pl
from jax.experimental.pallas import tpu as pltpu
from jax.sharding import PartitionSpec as P


LINE = 4
CHUNKS = (2, 3, 3, 2, 2)
SPLIT = 3
DIRECT = 1
SPAN = 32760.0
PAD = 16
SHIFT = 16
GRANT = 24 << 20
SLOTS = 64


def shifted(value, axis, offset):
    size = lax.axis_size(axis)
    return lax.ppermute(value, axis, [((i + offset) % size, i) for i in range(size)])


def member(value, near, offset):
    planes = lax.axis_size("depth") // near
    pairs = [
        (z * near + (y + offset) % near, z * near + y) for z in range(planes) for y in range(near)
    ]
    return lax.ppermute(value, "depth", pairs)


def hop(value, near, senders, flip):
    pairs = [(z * near + y, (z ^ flip) * near + y) for z in senders for y in range(near)]
    return lax.ppermute(value, "depth", pairs)


ALL = tuple(range(LINE))
EDGES = (0, LINE - 1)
INNER = tuple(range(1, LINE - 1))


def encode(total):
    peak = jnp.max(jnp.abs(total), axis=0, keepdims=True)
    level = jnp.ceil(jnp.log2(jnp.maximum(peak, 1e-30)) * 16.0)
    scaled = total * (jnp.exp2(level * (-1.0 / 16.0)) * SPAN)
    return jnp.round(scaled).astype(jnp.int32).astype(jnp.int16), level


def put_code(ref, at, cols, total):
    code, level = encode(total)
    rows = total.shape[0]
    ref[at : at + rows, cols] = code
    ref[at + rows : at + rows + PAD, cols] = (
        jnp.broadcast_to(level, (PAD, level.shape[1])).astype(jnp.int32).astype(jnp.int16)
    )


def decode(ref, at, cols, rows):
    level = ref[at + rows : at + rows + PAD, cols].astype(jnp.int32).astype(jnp.float32)[0:1]
    return ref[at : at + rows, cols].astype(jnp.int32).astype(jnp.float32) * (
        jnp.exp2(level * (1.0 / 16.0)) * (1.0 / SPAN)
    )


def tile_of(width):
    return 256 if width % 256 == 0 else 128


def tiled(width, fn):
    step = tile_of(width)

    def run(n, carry):
        fn(pl.ds(pl.multiple_of(n * step, step), step))
        return carry

    lax.fori_loop(0, width // step, run, 0)


def pick_kernel(grid, first, count, *refs):
    places, choose = refs[0], refs[1]
    raws = refs[2 : 2 + grid]
    outs = refs[2 + grid : -2]
    held, sems = refs[-2:]
    rows_dev, cols_dev = raws[0].shape[0], raws[0].shape[1]
    batch = math.gcd(count, 4)
    total = count * len(outs)

    def fetch(n, carry):
        slot = lax.bitwise_and(places[first + n], SLOTS - 1)
        for o in range(grid):
            @pl.when(lax.div(slot, rows_dev) == o)
            def _():
                held_row = raws[o].at[lax.rem(slot, rows_dev)]
                pltpu.make_async_copy(held_row, held.at[n], sems.at[n]).start()
        return carry

    lax.fori_loop(0, total, fetch, 0)
    low = lax.broadcasted_iota(jnp.int32, (64, 128), 1) < 64
    even = lax.broadcasted_iota(jnp.int32, (64, 128), 0) % 2 == 0
    same = low == even
    low_row = lax.broadcasted_iota(jnp.int32, (1, 128), 1) < 64

    def lay(s):
        def run(m, carry):
            stored = []
            for h in range(batch):
                n = s * count + m * batch + h
                pltpu.make_async_copy(raws[0].at[0], held.at[n], sems.at[n]).wait()
                x = held[n].astype(jnp.float32)
                parts = [x[:, 128 * i : 128 * (i + 1)] for i in range(32)]
                stored.append(jnp.concatenate(parts, axis=0).astype(jnp.bfloat16))
            spread = jnp.dot(
                choose[...],
                jnp.concatenate(stored, axis=1),
                preferred_element_type=jnp.float32,
            )
            for h in range(batch):
                t = m * batch + h
                place = places[first + s * count + t]
                for p in range(cols_dev // 2):
                    bit = jnp.where(low_row, SLOTS << (2 * p), SLOTS << (2 * p + 1))
                    live = (lax.bitwise_and(bit, place) != 0).astype(jnp.float32)
                    lanes = slice(128 * h, 128 * (h + 1))
                    top = spread[2 * p * 64 : (2 * p + 1) * 64, lanes]
                    under = spread[(2 * p + 1) * 64 : (2 * p + 2) * 64, lanes]
                    straight = jnp.where(low, top, under)
                    turned = pltpu.roll(jnp.where(low, under, top), 64, 1)
                    pair = jnp.where(same, straight, turned) * live
                    at = pl.ds(pl.multiple_of(t * 64, 64), 64)
                    outs[s][at, p * 128 : (p + 1) * 128] = pair.astype(jnp.bfloat16)
            return carry

        lax.fori_loop(0, count // batch, run, 0)

    for s in range(len(outs)):
        lay(s)


def pick(places, choose, raws, first, count, members):
    grid = len(raws)
    cols_dev, side2 = raws[0].shape[1:]
    total = count * members
    vmem = pl.BlockSpec(memory_space=pltpu.VMEM)
    shape = jax.ShapeDtypeStruct((count * 64, cols_dev * 64), jnp.bfloat16)
    return pl.pallas_call(
        functools.partial(pick_kernel, grid, first, count),
        out_shape=[shape] * members,
        in_specs=[pl.BlockSpec(memory_space=pltpu.SMEM), vmem]
        + [pl.BlockSpec(memory_space=pl.ANY)] * grid,
        out_specs=[vmem] * members,
        scratch_shapes=[
            pltpu.VMEM((total, cols_dev, side2), jnp.bfloat16),
            pltpu.SemaphoreType.DMA((total,)),
        ],
        compiler_params=pltpu.CompilerParams(vmem_limit_bytes=GRANT),
        cost_estimate=pl.CostEstimate(
            flops=0, transcendentals=0, bytes_accessed=4 * total * cols_dev * side2
        ),
        name="pick",
    )(places, choose, *raws)


def cut_kernel(widths, begin, wide, mask, b, *outs):
    blocks = mask.shape[0]
    shape = (mask.shape[1], b.shape[1])
    expand = (
        lax.broadcasted_iota(jnp.int32, shape, 1) // 64
        == lax.broadcasted_iota(jnp.int32, shape, 0)
    ).astype(jnp.float32)
    live = jnp.dot(
        mask[...].astype(jnp.float32), expand, preferred_element_type=jnp.float32
    ).astype(jnp.bfloat16)
    spans = [(sum(widths[:i]) + begin, w, outs[i]) for i, w in enumerate(widths)]
    if wide:
        spans = [(0, begin, None)] + spans
    for s in range(blocks):
        rows = slice(s * 64, (s + 1) * 64)
        for start, width, out in spans:
            cols = slice(start, start + width)
            kept = b[rows, cols] * live[s : s + 1, cols]
            if out is not None:
                out[rows, :] = kept
            if wide:
                outs[-1][rows, cols] = kept


def cut(b_matrix, b_mask, widths, begin, wide):
    vmem = pl.BlockSpec(memory_space=pltpu.VMEM)
    rows, full = b_matrix.shape
    read = full if wide else begin + sum(widths)
    outs = [*widths, full] if wide else widths

    def whole(shape):
        return pl.BlockSpec(shape, lambda i: (0, 0))

    return pl.pallas_call(
        functools.partial(cut_kernel, widths, begin, wide),
        grid=(1,),
        out_shape=[jax.ShapeDtypeStruct((rows, w), jnp.bfloat16) for w in outs],
        in_specs=[whole(b_mask.shape), whole((rows, read))],
        out_specs=[whole((rows, w)) for w in outs],
        cost_estimate=pl.CostEstimate(
            flops=0, transcendentals=0, bytes_accessed=6 * rows * read
        ),
        compiler_params=pltpu.CompilerParams(vmem_limit_bytes=GRANT),
        name="cut",
    )(b_mask, b_matrix)


def multiply_kernel(grid, planes_y, lows, direct, start, *refs):
    table = refs[0]
    count = grid * planes_y
    total_in = count * len(lows)
    lefts = [refs[1 + i * count : 1 + (i + 1) * count] for i in range(len(lows))]
    rights = refs[1 + total_in : 1 + total_in + count]
    outs = refs[1 + total_in + count : -2]
    right, right_sems = refs[-2:]
    piece = lefts[0][0].shape[1]
    cols_dev = piece // 64
    width = right.shape[1]
    rows = lefts[0][0].shape[0] // 2
    step = tile_of(width)
    for n in range(width // step):
        for q in range(count):
            begin = n * step + (0 if q % planes_y else start)
            for w in range(cols_dev):
                row = q * cols_dev + w
                code = table[row]
                at = pl.ds(pl.multiple_of(lax.bitwise_and(code, (1 << SHIFT) - 1), 64), 64)
                for o in range(grid):
                    @pl.when(lax.shift_right_logical(code, SHIFT) == o)
                    def _():
                        pltpu.make_async_copy(
                            rights[o * planes_y + q % planes_y].at[at, begin : begin + step],
                            right.at[row * 64 : (row + 1) * 64, n * step : (n + 1) * step],
                            right_sems.at[n],
                        ).start()

    def run(n, carry):
        cols = pl.ds(pl.multiple_of(n * step, step), step)
        held = right.at[:, cols]
        pltpu.make_async_copy(held, held, right_sems.at[n]).wait()
        for i in range(2 * len(lows)):
            g = lows[i // 2] + i % 2
            same = slice(i % 2 * rows, (i % 2 + 1) * rows)
            total = None
            for q in range(count):
                more = jnp.dot(
                    lefts[i // 2][q][same, :],
                    right[q * piece : (q + 1) * piece, cols],
                    preferred_element_type=jnp.float32,
                )
                total = more if total is None else total + more
            if g < 2 and direct:
                put_code(outs[g], 0, cols, total)
            elif g < 2:
                outs[1][same, cols] = total
                put_code(outs[0], g * (rows + PAD), cols, total)
            elif g == 2:
                put_code(outs[-2], 0, cols, total)
            else:
                outs[-1][:, cols] = total
        return carry

    lax.fori_loop(0, width // step, run, 0)


def multiply(table, lefts, rights, lows, direct, grid, planes_y, start, width):
    part_rows, piece = lefts[0][0].shape
    rows = part_rows // 2
    inner = piece * len(lefts[0])
    all_rows = part_rows * len(lows)
    code = jax.ShapeDtypeStruct((rows + PAD, width), jnp.int16)
    outs = []
    if 0 in lows and direct:
        outs += [code, code]
    elif 0 in lows:
        outs += [
            jax.ShapeDtypeStruct((2 * (rows + PAD), width), jnp.int16),
            jax.ShapeDtypeStruct((2 * rows, width), jnp.float32),
        ]
    if 2 in lows:
        outs += [code, jax.ShapeDtypeStruct((rows, width), jnp.float32)]
    hbm = pl.BlockSpec(memory_space=pl.ANY)
    vmem = pl.BlockSpec(memory_space=pltpu.VMEM)
    arrays = [v for part in lefts for v in part]
    return pl.pallas_call(
        functools.partial(multiply_kernel, grid, planes_y, lows, direct, start),
        out_shape=outs,
        in_specs=[pl.BlockSpec(memory_space=pltpu.SMEM)]
        + [vmem] * len(arrays)
        + [hbm] * len(rights),
        out_specs=[vmem] * len(outs),
        scratch_shapes=[
            pltpu.VMEM((inner, width), jnp.bfloat16),
            pltpu.SemaphoreType.DMA((width // tile_of(width),)),
        ],
        compiler_params=pltpu.CompilerParams(vmem_limit_bytes=GRANT),
        cost_estimate=pl.CostEstimate(
            flops=2 * all_rows * inner * width,
            transcendentals=0,
            bytes_accessed=2 * inner * (all_rows + width) + 6 * all_rows * width,
        ),
        name="multiply",
    )(table, *arrays, *rights)


def relay_kernel(own, code, three, two):
    rows = three.shape[0] - PAD

    def run(cols):
        total = own[0:rows, cols] + decode(code, rows + PAD, cols, rows)
        put_code(three, 0, cols, total)
        total = own[rows : 2 * rows, cols] + decode(code, 0, cols, rows)
        put_code(two, 0, cols, total)

    tiled(own.shape[1], run)


def relay(own, code):
    vmem = pl.BlockSpec(memory_space=pltpu.VMEM)
    out = jax.ShapeDtypeStruct((code.shape[0] // 2, code.shape[1]), code.dtype)
    return pl.pallas_call(
        relay_kernel,
        out_shape=[out, out],
        in_specs=[vmem, vmem],
        out_specs=[vmem, vmem],
        cost_estimate=pl.CostEstimate(
            flops=0, transcendentals=0, bytes_accessed=8 * own.size
        ),
        compiler_params=pltpu.CompilerParams(vmem_limit_bytes=GRANT),
        name="relay",
    )(own, code)


def finish_kernel(start, own, *refs):
    codes, out, stage, sem = refs[:3], refs[-3], refs[-2], refs[-1]
    rows, width = own.shape

    def run(cols):
        total = own[:, cols]
        for code in codes:
            total = total + decode(code, 0, cols, rows)
        stage[:, cols] = total.astype(jnp.bfloat16)

    tiled(width, run)
    copy = pltpu.make_async_copy(stage, out.at[:, start : start + width], sem)
    copy.start()
    copy.wait()


def finish(own, codes, start, full, so_far):
    vmem = pl.BlockSpec(memory_space=pltpu.VMEM)
    hbm = pl.BlockSpec(memory_space=pltpu.HBM)
    operands = [own, *codes]
    specs = [vmem] * len(operands)
    aliases = {}
    if so_far is not None:
        aliases = {len(operands): 0}
        operands.append(so_far)
        specs.append(hbm)
    return pl.pallas_call(
        functools.partial(finish_kernel, start),
        out_shape=jax.ShapeDtypeStruct((own.shape[0], full), jnp.bfloat16),
        in_specs=specs,
        out_specs=hbm,
        scratch_shapes=[pltpu.VMEM(own.shape, jnp.bfloat16), pltpu.SemaphoreType.DMA(())],
        input_output_aliases=aliases,
        cost_estimate=pl.CostEstimate(
            flops=0, transcendentals=0, bytes_accessed=12 * own.size
        ),
        compiler_params=pltpu.CompilerParams(vmem_limit_bytes=GRANT),
        name="finish",
    )(*operands)


def body(a_blocks, a_mask, a_row_ids, a_col_ids, b_matrix, b_mask):
    grid = lax.axis_size("row")
    depth = lax.axis_size("depth")
    planes_y = depth // LINE
    rows_dev, cols_dev = a_blocks.shape[:2]
    home_rows = rows_dev // depth
    full = b_matrix.shape[1]
    unit = full // sum(CHUNKS)
    widths = [unit * c for c in CHUNKS]
    starts = [sum(widths[:j]) for j in range(len(widths))]

    my_row, my_col = lax.axis_index("row"), lax.axis_index("col")
    my_depth = lax.axis_index("depth")
    my_line, my_near = my_depth // planes_y, my_depth % planes_y
    n = jnp.arange(grid * planes_y * cols_dev, dtype=jnp.int32)
    piece = n // cols_dev
    holder = (my_col + piece // planes_y) % grid * depth
    holder = holder + my_line * planes_y + (my_near + piece % planes_y) % planes_y
    column = holder * cols_dev + n % cols_dev
    every = jnp.arange(a_col_ids.shape[0], dtype=jnp.int32)
    k = jnp.sum(jnp.where(every[None, :] == column[:, None], a_col_ids[None, :], 0), axis=1)
    shift = (k // (cols_dev * depth) - my_row + grid) % grid
    table = shift * (1 << SHIFT) + k % cols_dev * 64
    to = lax.broadcasted_iota(jnp.int32, (cols_dev * 64, cols_dev * 32), 0)
    come = lax.broadcasted_iota(jnp.int32, (cols_dev * 64, cols_dev * 32), 1)
    choose = (come == to % 64 // 2 * cols_dev + to // 64).astype(jnp.bfloat16)

    raws = [a_blocks] + [shifted(a_blocks, "row", o) for o in range(1, grid)]
    masks = [a_mask] + [shifted(a_mask, "row", o) for o in range(1, grid)]
    count = 2 * home_rows
    n = jnp.arange(4 * home_rows * planes_y, dtype=jnp.int32)
    low, rest = n // (count * planes_y) * 2, n % (count * planes_y)
    ahead = (rest // count + 1) % planes_y
    line = my_line ^ (LINE - 1 - low - rest % count // home_rows)
    block = (my_row * depth + line * planes_y + (my_near - ahead) % planes_y) * home_rows
    block = block + n % home_rows
    turned = lax.dynamic_slice(
        jnp.concatenate([a_row_ids, a_row_ids]), (my_row * rows_dev,), a_row_ids.shape
    )
    bits = jnp.concatenate(masks) << jnp.arange(cols_dev, dtype=jnp.int32)[None, :]
    entry = jnp.arange(grid * rows_dev, dtype=jnp.int32) + SLOTS * jnp.sum(bits, axis=1)
    places = jnp.sum(jnp.where(turned[None, :] == block[:, None], entry[None, :], 0), axis=1)
    early = cut(b_matrix, b_mask, widths[:1], 0, False)
    *later, whole = cut(b_matrix, b_mask, widths[1:], widths[0], True)
    cuts = [*early, *later]
    wholes = [whole] + [shifted(whole, "row", o) for o in range(1, grid)]

    parts = []
    for n in range(2):
        first = n * count * planes_y
        picked = list(pick(places, choose, raws, first, count, planes_y - 1))
        first += count * (planes_y - 1)
        near = list(pick(places, choose, raws, first, count, 1)) + picked
        near = [member(v, planes_y, s) if s else v for s, v in enumerate(near)]
        far = []
        for x in range(1, grid):
            for v in near:
                far.append(shifted(v, "col", x))
        parts.append(near + far)

    product = None
    for j, (start, width, mine) in enumerate(zip(starts, widths, cuts)):
        direct = j >= len(widths) - DIRECT
        near = [member(mine, planes_y, s) for s in range(1, planes_y)]
        rights = [wholes[0]] + near
        for o in range(1, grid):
            rights += [wholes[o]] + [shifted(v, "row", o) for v in near]
        got = []
        for n, lows in enumerate(((0,), (2,)) if j < SPLIT else ((0, 2),)):
            got += multiply(
                table,
                [parts[low // 2] for low in lows],
                rights,
                lows,
                direct,
                grid,
                planes_y,
                start,
                width,
            )
        first, second, beside, own = got
        if direct:
            codes = [hop(first, planes_y, ALL, 3), hop(second, planes_y, ALL, 2)]
        else:
            came = hop(first, planes_y, EDGES, 1)
            three, two = relay(second, came)
            codes = [hop(three, planes_y, INNER, 3), hop(two, planes_y, INNER, 2)]
        codes.append(hop(beside, planes_y, ALL, 1))
        product = finish(own, codes, start, full, product)
    return product


def solution(mesh):
    return jax.shard_map(
        body,
        mesh=mesh,
        in_specs=(
            P("row", ("col", "depth"), None),
            P("row", ("col", "depth")),
            P(),
            P(),
            P(("row", "depth"), "col"),
            P(("row", "depth"), "col"),
        ),
        out_specs=P(("row", "depth"), "col"),
        check_vma=False,
    )
```

```python
import functools
import math

import jax
import jax.numpy as jnp
from jax import lax
from jax.experimental import pallas as pl
from jax.experimental.pallas import tpu as pltpu
from jax.sharding import PartitionSpec as P


LINE = 4
CHUNKS = (2, 3, 3, 2, 2)
DIRECT = 1
SPAN = 32760.0
PAD = 8
SHIFT = 16
GRANT = 24 << 20
SLOTS = 64


def shifted(value, axis, offset):
    size = lax.axis_size(axis)
    return lax.ppermute(value, axis, [((i + offset) % size, i) for i in range(size)])


def member(value, near, offset):
    planes = lax.axis_size("depth") // near
    pairs = [
        (z * near + (y + offset) % near, z * near + y) for z in range(planes) for y in range(near)
    ]
    return lax.ppermute(value, "depth", pairs)


def hop(value, near, senders, flip):
    pairs = [(z * near + y, (z ^ flip) * near + y) for z in senders for y in range(near)]
    return lax.ppermute(value, "depth", pairs)


ALL = tuple(range(LINE))
EDGES = (0, LINE - 1)
INNER = tuple(range(1, LINE - 1))


def encode(total):
    peak = jnp.max(jnp.abs(total), axis=0, keepdims=True)
    level = jnp.ceil(jnp.log2(jnp.maximum(peak, 1e-30)) * 16.0)
    scaled = total * (jnp.exp2(level * (-1.0 / 16.0)) * SPAN)
    return jnp.round(scaled).astype(jnp.int32).astype(jnp.int16), level


def put_code(ref, at, cols, total):
    code, level = encode(total)
    rows = total.shape[0]
    ref[at : at + rows, cols] = code
    ref[at + rows : at + rows + PAD, cols] = (
        jnp.broadcast_to(level, (PAD, level.shape[1])).astype(jnp.int32).astype(jnp.int16)
    )


def decode(ref, at, cols, rows):
    level = ref[at + rows : at + rows + PAD, cols].astype(jnp.int32).astype(jnp.float32)[0:1]
    return ref[at : at + rows, cols].astype(jnp.int32).astype(jnp.float32) * (
        jnp.exp2(level * (1.0 / 16.0)) * (1.0 / SPAN)
    )


def tile_of(width):
    return 256 if width % 256 == 0 else 128


def tiled(width, fn):
    step = tile_of(width)

    def run(n, carry):
        fn(pl.ds(pl.multiple_of(n * step, step), step))
        return carry

    lax.fori_loop(0, width // step, run, 0)


def pick_kernel(grid, first, count, *refs):
    places, choose = refs[0], refs[1]
    raws = refs[2 : 2 + grid]
    outs = refs[2 + grid : -2]
    held, sems = refs[-2:]
    rows_dev, cols_dev = raws[0].shape[0], raws[0].shape[1]
    batch = math.gcd(count, 4)
    total = count * len(outs)

    def fetch(n, carry):
        slot = lax.bitwise_and(places[first + n], SLOTS - 1)
        for o in range(grid):
            @pl.when(lax.div(slot, rows_dev) == o)
            def _():
                held_row = raws[o].at[lax.rem(slot, rows_dev)]
                pltpu.make_async_copy(held_row, held.at[n], sems.at[n]).start()
        return carry

    lax.fori_loop(0, total, fetch, 0)
    low = lax.broadcasted_iota(jnp.int32, (64, 128), 1) < 64
    even = lax.broadcasted_iota(jnp.int32, (64, 128), 0) % 2 == 0
    same = low == even
    low_row = lax.broadcasted_iota(jnp.int32, (1, 128), 1) < 64

    def lay(s):
        def run(m, carry):
            stored = []
            for h in range(batch):
                n = s * count + m * batch + h
                pltpu.make_async_copy(raws[0].at[0], held.at[n], sems.at[n]).wait()
                x = held[n].astype(jnp.float32)
                parts = [x[:, 128 * i : 128 * (i + 1)] for i in range(32)]
                stored.append(jnp.concatenate(parts, axis=0).astype(jnp.bfloat16))
            spread = jnp.dot(
                choose[...],
                jnp.concatenate(stored, axis=1),
                preferred_element_type=jnp.float32,
            )
            for h in range(batch):
                t = m * batch + h
                place = places[first + s * count + t]
                for p in range(cols_dev // 2):
                    bit = jnp.where(low_row, SLOTS << (2 * p), SLOTS << (2 * p + 1))
                    live = (lax.bitwise_and(bit, place) != 0).astype(jnp.float32)
                    lanes = slice(128 * h, 128 * (h + 1))
                    top = spread[2 * p * 64 : (2 * p + 1) * 64, lanes]
                    under = spread[(2 * p + 1) * 64 : (2 * p + 2) * 64, lanes]
                    straight = jnp.where(low, top, under)
                    turned = pltpu.roll(jnp.where(low, under, top), 64, 1)
                    pair = jnp.where(same, straight, turned) * live
                    at = pl.ds(pl.multiple_of(t * 64, 64), 64)
                    outs[s][at, p * 128 : (p + 1) * 128] = pair.astype(jnp.bfloat16)
            return carry

        lax.fori_loop(0, count // batch, run, 0)

    for s in range(len(outs)):
        lay(s)


def pick(places, choose, raws, first, count, members):
    grid = len(raws)
    cols_dev, side2 = raws[0].shape[1:]
    total = count * members
    vmem = pl.BlockSpec(memory_space=pltpu.VMEM)
    shape = jax.ShapeDtypeStruct((count * 64, cols_dev * 64), jnp.bfloat16)
    return pl.pallas_call(
        functools.partial(pick_kernel, grid, first, count),
        out_shape=[shape] * members,
        in_specs=[pl.BlockSpec(memory_space=pltpu.SMEM), vmem]
        + [pl.BlockSpec(memory_space=pl.ANY)] * grid,
        out_specs=[vmem] * members,
        scratch_shapes=[
            pltpu.VMEM((total, cols_dev, side2), jnp.bfloat16),
            pltpu.SemaphoreType.DMA((total,)),
        ],
        compiler_params=pltpu.CompilerParams(vmem_limit_bytes=GRANT),
        cost_estimate=pl.CostEstimate(
            flops=0, transcendentals=0, bytes_accessed=4 * total * cols_dev * side2
        ),
        name="pick",
    )(places, choose, *raws)


def cut_kernel(widths, begin, wide, mask, b, *outs):
    blocks = mask.shape[0]
    shape = (mask.shape[1], b.shape[1])
    expand = (
        lax.broadcasted_iota(jnp.int32, shape, 1) // 64
        == lax.broadcasted_iota(jnp.int32, shape, 0)
    ).astype(jnp.float32)
    live = jnp.dot(
        mask[...].astype(jnp.float32), expand, preferred_element_type=jnp.float32
    ).astype(jnp.bfloat16)
    spans = [(sum(widths[:i]) + begin, w, outs[i]) for i, w in enumerate(widths)]
    if wide:
        spans = [(0, begin, None)] + spans
    for s in range(blocks):
        rows = slice(s * 64, (s + 1) * 64)
        for start, width, out in spans:
            cols = slice(start, start + width)
            kept = b[rows, cols] * live[s : s + 1, cols]
            if out is not None:
                out[rows, :] = kept
            if wide:
                outs[-1][rows, cols] = kept


def cut(b_matrix, b_mask, widths, begin, wide):
    vmem = pl.BlockSpec(memory_space=pltpu.VMEM)
    rows, full = b_matrix.shape
    read = full if wide else begin + sum(widths)
    outs = [*widths, full] if wide else widths

    def whole(shape):
        return pl.BlockSpec(shape, lambda i: (0, 0))

    return pl.pallas_call(
        functools.partial(cut_kernel, widths, begin, wide),
        grid=(1,),
        out_shape=[jax.ShapeDtypeStruct((rows, w), jnp.bfloat16) for w in outs],
        in_specs=[whole(b_mask.shape), whole((rows, read))],
        out_specs=[whole((rows, w)) for w in outs],
        cost_estimate=pl.CostEstimate(
            flops=0, transcendentals=0, bytes_accessed=6 * rows * read
        ),
        compiler_params=pltpu.CompilerParams(vmem_limit_bytes=GRANT),
        name="cut",
    )(b_mask, b_matrix)


def multiply_kernel(grid, planes_y, lows, direct, start, *refs):
    table = refs[0]
    count = grid * planes_y
    total_in = count * len(lows)
    lefts = [refs[1 + i * count : 1 + (i + 1) * count] for i in range(len(lows))]
    rights = refs[1 + total_in : 1 + total_in + count]
    outs = refs[1 + total_in + count : -2]
    right, right_sems = refs[-2:]
    piece = lefts[0][0].shape[1]
    cols_dev = piece // 64
    width = right.shape[1]
    rows = lefts[0][0].shape[0] // 2
    step = tile_of(width)
    for n in range(width // step):
        for q in range(count):
            begin = n * step + (0 if q % planes_y else start)
            for w in range(cols_dev):
                row = q * cols_dev + w
                code = table[row]
                at = pl.ds(pl.multiple_of(lax.bitwise_and(code, (1 << SHIFT) - 1), 64), 64)
                for o in range(grid):
                    @pl.when(lax.shift_right_logical(code, SHIFT) == o)
                    def _():
                        pltpu.make_async_copy(
                            rights[o * planes_y + q % planes_y].at[at, begin : begin + step],
                            right.at[row * 64 : (row + 1) * 64, n * step : (n + 1) * step],
                            right_sems.at[n],
                        ).start()

    def run(n, carry):
        cols = pl.ds(pl.multiple_of(n * step, step), step)
        held = right.at[:, cols]
        pltpu.make_async_copy(held, held, right_sems.at[n]).wait()
        for i in range(2 * len(lows)):
            g = lows[i // 2] + i % 2
            same = slice(i % 2 * rows, (i % 2 + 1) * rows)
            total = None
            for q in range(count):
                more = jnp.dot(
                    lefts[i // 2][q][same, :],
                    right[q * piece : (q + 1) * piece, cols],
                    preferred_element_type=jnp.float32,
                )
                total = more if total is None else total + more
            if g < 2 and direct:
                put_code(outs[g], 0, cols, total)
            elif g < 2:
                outs[1][same, cols] = total
                put_code(outs[0], g * (rows + PAD), cols, total)
            elif g == 2:
                put_code(outs[-2], 0, cols, total)
            else:
                outs[-1][:, cols] = total
        return carry

    lax.fori_loop(0, width // step, run, 0)


def multiply(table, lefts, rights, lows, direct, grid, planes_y, start, width):
    part_rows, piece = lefts[0][0].shape
    rows = part_rows // 2
    inner = piece * len(lefts[0])
    all_rows = part_rows * len(lows)
    code = jax.ShapeDtypeStruct((rows + PAD, width), jnp.int16)
    outs = []
    if 0 in lows and direct:
        outs += [code, code]
    elif 0 in lows:
        outs += [
            jax.ShapeDtypeStruct((2 * (rows + PAD), width), jnp.int16),
            jax.ShapeDtypeStruct((2 * rows, width), jnp.float32),
        ]
    if 2 in lows:
        outs += [code, jax.ShapeDtypeStruct((rows, width), jnp.float32)]
    hbm = pl.BlockSpec(memory_space=pl.ANY)
    vmem = pl.BlockSpec(memory_space=pltpu.VMEM)
    arrays = [v for part in lefts for v in part]
    return pl.pallas_call(
        functools.partial(multiply_kernel, grid, planes_y, lows, direct, start),
        out_shape=outs,
        in_specs=[pl.BlockSpec(memory_space=pltpu.SMEM)]
        + [vmem] * len(arrays)
        + [hbm] * len(rights),
        out_specs=[vmem] * len(outs),
        scratch_shapes=[
            pltpu.VMEM((inner, width), jnp.bfloat16),
            pltpu.SemaphoreType.DMA((width // tile_of(width),)),
        ],
        compiler_params=pltpu.CompilerParams(vmem_limit_bytes=GRANT),
        cost_estimate=pl.CostEstimate(
            flops=2 * all_rows * inner * width,
            transcendentals=0,
            bytes_accessed=2 * inner * (all_rows + width) + 6 * all_rows * width,
        ),
        name="multiply",
    )(table, *arrays, *rights)


def relay_kernel(own, code, three, two):
    rows = three.shape[0] - PAD

    def run(cols):
        total = own[0:rows, cols] + decode(code, rows + PAD, cols, rows)
        put_code(three, 0, cols, total)
        total = own[rows : 2 * rows, cols] + decode(code, 0, cols, rows)
        put_code(two, 0, cols, total)

    tiled(own.shape[1], run)


def relay(own, code):
    vmem = pl.BlockSpec(memory_space=pltpu.VMEM)
    out = jax.ShapeDtypeStruct((code.shape[0] // 2, code.shape[1]), code.dtype)
    return pl.pallas_call(
        relay_kernel,
        out_shape=[out, out],
        in_specs=[vmem, vmem],
        out_specs=[vmem, vmem],
        cost_estimate=pl.CostEstimate(
            flops=0, transcendentals=0, bytes_accessed=8 * own.size
        ),
        compiler_params=pltpu.CompilerParams(vmem_limit_bytes=GRANT),
        name="relay",
    )(own, code)


def finish_kernel(start, own, *refs):
    codes, out, stage, sem = refs[:3], refs[-3], refs[-2], refs[-1]
    rows, width = own.shape

    def run(cols):
        total = own[:, cols]
        for code in codes:
            total = total + decode(code, 0, cols, rows)
        stage[:, cols] = total.astype(jnp.bfloat16)

    tiled(width, run)
    copy = pltpu.make_async_copy(stage, out.at[:, start : start + width], sem)
    copy.start()
    copy.wait()


def finish(own, codes, start, full, so_far):
    vmem = pl.BlockSpec(memory_space=pltpu.VMEM)
    hbm = pl.BlockSpec(memory_space=pltpu.HBM)
    operands = [own, *codes]
    specs = [vmem] * len(operands)
    aliases = {}
    if so_far is not None:
        aliases = {len(operands): 0}
        operands.append(so_far)
        specs.append(hbm)
    return pl.pallas_call(
        functools.partial(finish_kernel, start),
        out_shape=jax.ShapeDtypeStruct((own.shape[0], full), jnp.bfloat16),
        in_specs=specs,
        out_specs=hbm,
        scratch_shapes=[pltpu.VMEM(own.shape, jnp.bfloat16), pltpu.SemaphoreType.DMA(())],
        input_output_aliases=aliases,
        cost_estimate=pl.CostEstimate(
            flops=0, transcendentals=0, bytes_accessed=12 * own.size
        ),
        compiler_params=pltpu.CompilerParams(vmem_limit_bytes=GRANT),
        name="finish",
    )(*operands)


def body(a_blocks, a_mask, a_row_ids, a_col_ids, b_matrix, b_mask):
    grid = lax.axis_size("row")
    depth = lax.axis_size("depth")
    planes_y = depth // LINE
    rows_dev, cols_dev = a_blocks.shape[:2]
    home_rows = rows_dev // depth
    full = b_matrix.shape[1]
    unit = full // sum(CHUNKS)
    widths = [unit * c for c in CHUNKS]
    starts = [sum(widths[:j]) for j in range(len(widths))]

    my_row, my_col = lax.axis_index("row"), lax.axis_index("col")
    my_depth = lax.axis_index("depth")
    my_line, my_near = my_depth // planes_y, my_depth % planes_y
    n = jnp.arange(grid * planes_y * cols_dev, dtype=jnp.int32)
    piece = n // cols_dev
    holder = (my_col + piece // planes_y) % grid * depth
    holder = holder + my_line * planes_y + (my_near + piece % planes_y) % planes_y
    column = holder * cols_dev + n % cols_dev
    every = jnp.arange(a_col_ids.shape[0], dtype=jnp.int32)
    k = jnp.sum(jnp.where(every[None, :] == column[:, None], a_col_ids[None, :], 0), axis=1)
    shift = (k // (cols_dev * depth) - my_row + grid) % grid
    table = shift * (1 << SHIFT) + k % cols_dev * 64
    to = lax.broadcasted_iota(jnp.int32, (cols_dev * 64, cols_dev * 32), 0)
    come = lax.broadcasted_iota(jnp.int32, (cols_dev * 64, cols_dev * 32), 1)
    choose = (come == to % 64 // 2 * cols_dev + to // 64).astype(jnp.bfloat16)

    raws = [a_blocks] + [shifted(a_blocks, "row", o) for o in range(1, grid)]
    masks = [a_mask] + [shifted(a_mask, "row", o) for o in range(1, grid)]
    count = 2 * home_rows
    n = jnp.arange(4 * home_rows * planes_y, dtype=jnp.int32)
    low, rest = n // (count * planes_y) * 2, n % (count * planes_y)
    ahead = (rest // count + 1) % planes_y
    line = my_line ^ (LINE - 1 - low - rest % count // home_rows)
    block = (my_row * depth + line * planes_y + (my_near - ahead) % planes_y) * home_rows
    block = block + n % home_rows
    turned = lax.dynamic_slice(
        jnp.concatenate([a_row_ids, a_row_ids]), (my_row * rows_dev,), a_row_ids.shape
    )
    bits = jnp.concatenate(masks) << jnp.arange(cols_dev, dtype=jnp.int32)[None, :]
    entry = jnp.arange(grid * rows_dev, dtype=jnp.int32) + SLOTS * jnp.sum(bits, axis=1)
    places = jnp.sum(jnp.where(turned[None, :] == block[:, None], entry[None, :], 0), axis=1)
    early = cut(b_matrix, b_mask, widths[:1], 0, False)
    *later, whole = cut(b_matrix, b_mask, widths[1:], widths[0], True)
    cuts = [*early, *later]
    wholes = [whole] + [shifted(whole, "row", o) for o in range(1, grid)]

    parts = []
    for n in range(2):
        first = n * count * planes_y
        picked = list(pick(places, choose, raws, first, count, planes_y - 1))
        first += count * (planes_y - 1)
        near = list(pick(places, choose, raws, first, count, 1)) + picked
        near = [member(v, planes_y, s) if s else v for s, v in enumerate(near)]
        far = []
        for x in range(1, grid):
            for v in near:
                far.append(shifted(v, "col", x))
        parts.append(near + far)

    product = None
    for j, (start, width, mine) in enumerate(zip(starts, widths, cuts)):
        direct = j < DIRECT
        near = [member(mine, planes_y, s) for s in range(1, planes_y)]
        rights = [wholes[0]] + near
        for o in range(1, grid):
            rights += [wholes[o]] + [shifted(v, "row", o) for v in near]
        got = []
        for n, lows in enumerate(((0,), (2,))):
            got += multiply(
                table,
                [parts[low // 2] for low in lows],
                rights,
                lows,
                direct,
                grid,
                planes_y,
                start,
                width,
            )
        first, second, beside, own = got
        if direct:
            codes = [hop(first, planes_y, ALL, 3), hop(second, planes_y, ALL, 2)]
        else:
            came = hop(first, planes_y, EDGES, 1)
            three, two = relay(second, came)
            codes = [hop(three, planes_y, INNER, 3), hop(two, planes_y, INNER, 2)]
        codes.append(hop(beside, planes_y, ALL, 1))
        product = finish(own, codes, start, full, product)
    return product


def solution(mesh):
    return jax.shard_map(
        body,
        mesh=mesh,
        in_specs=(
            P("row", ("col", "depth"), None),
            P("row", ("col", "depth")),
            P(),
            P(),
            P(("row", "depth"), "col"),
            P(("row", "depth"), "col"),
        ),
        out_specs=P(("row", "depth"), "col"),
        check_vma=False,
    )
```

```python
import functools
import math

import jax
import jax.numpy as jnp
from jax import lax
from jax.experimental import pallas as pl
from jax.experimental.pallas import tpu as pltpu
from jax.sharding import PartitionSpec as P


LINE = 4
CHUNKS = (2, 3, 3, 3, 1)
DIRECT = 1
NEAR = ((0, 1), (2,), (3, 4))
SPAN = 32760.0
PAD = 8
SHIFT = 16
GRANT = 24 << 20
SLOTS = 64


def shifted(value, axis, offset):
    size = lax.axis_size(axis)
    return lax.ppermute(value, axis, [((i + offset) % size, i) for i in range(size)])


def member(value, near, offset):
    planes = lax.axis_size("depth") // near
    pairs = [
        (z * near + (y + offset) % near, z * near + y) for z in range(planes) for y in range(near)
    ]
    return lax.ppermute(value, "depth", pairs)


def hop(value, near, senders, flip):
    pairs = [(z * near + y, (z ^ flip) * near + y) for z in senders for y in range(near)]
    return lax.ppermute(value, "depth", pairs)


ALL = tuple(range(LINE))
EDGES = (0, LINE - 1)
INNER = tuple(range(1, LINE - 1))


def encode(total):
    peak = jnp.max(jnp.abs(total), axis=0, keepdims=True)
    level = jnp.ceil(jnp.log2(jnp.maximum(peak, 1e-30)) * 16.0)
    scaled = total * (jnp.exp2(level * (-1.0 / 16.0)) * SPAN)
    return jnp.round(scaled).astype(jnp.int32).astype(jnp.int16), level


def put_code(ref, at, cols, total):
    code, level = encode(total)
    rows = total.shape[0]
    ref[at : at + rows, cols] = code
    ref[at + rows : at + rows + PAD, cols] = (
        jnp.broadcast_to(level, (PAD, level.shape[1])).astype(jnp.int32).astype(jnp.int16)
    )


def decode(ref, at, cols, rows):
    level = ref[at + rows : at + rows + PAD, cols].astype(jnp.int32).astype(jnp.float32)[0:1]
    return ref[at : at + rows, cols].astype(jnp.int32).astype(jnp.float32) * (
        jnp.exp2(level * (1.0 / 16.0)) * (1.0 / SPAN)
    )


def tile_of(width):
    return 256 if width % 256 == 0 else 128


def tiled(width, fn):
    step = tile_of(width)

    def run(n, carry):
        fn(pl.ds(pl.multiple_of(n * step, step), step))
        return carry

    lax.fori_loop(0, width // step, run, 0)


def pick_kernel(grid, first, count, *refs):
    places, choose = refs[0], refs[1]
    raws = refs[2 : 2 + grid]
    outs = refs[2 + grid : -2]
    held, sems = refs[-2:]
    rows_dev, cols_dev = raws[0].shape[0], raws[0].shape[1]
    batch = math.gcd(count, 4)
    total = count * len(outs)

    def fetch(n, carry):
        slot = lax.bitwise_and(places[first + n], SLOTS - 1)
        for o in range(grid):
            @pl.when(lax.div(slot, rows_dev) == o)
            def _():
                held_row = raws[o].at[lax.rem(slot, rows_dev)]
                pltpu.make_async_copy(held_row, held.at[n], sems.at[n]).start()
        return carry

    lax.fori_loop(0, total, fetch, 0)
    low = lax.broadcasted_iota(jnp.int32, (64, 128), 1) < 64
    even = lax.broadcasted_iota(jnp.int32, (64, 128), 0) % 2 == 0
    same = low == even
    low_row = lax.broadcasted_iota(jnp.int32, (1, 128), 1) < 64

    def lay(s):
        def run(m, carry):
            stored = []
            for h in range(batch):
                n = s * count + m * batch + h
                pltpu.make_async_copy(raws[0].at[0], held.at[n], sems.at[n]).wait()
                x = held[n].astype(jnp.float32)
                parts = [x[:, 128 * i : 128 * (i + 1)] for i in range(32)]
                stored.append(jnp.concatenate(parts, axis=0).astype(jnp.bfloat16))
            spread = jnp.dot(
                choose[...],
                jnp.concatenate(stored, axis=1),
                preferred_element_type=jnp.float32,
            )
            for h in range(batch):
                t = m * batch + h
                place = places[first + s * count + t]
                for p in range(cols_dev // 2):
                    bit = jnp.where(low_row, SLOTS << (2 * p), SLOTS << (2 * p + 1))
                    live = (lax.bitwise_and(bit, place) != 0).astype(jnp.float32)
                    lanes = slice(128 * h, 128 * (h + 1))
                    top = spread[2 * p * 64 : (2 * p + 1) * 64, lanes]
                    under = spread[(2 * p + 1) * 64 : (2 * p + 2) * 64, lanes]
                    straight = jnp.where(low, top, under)
                    turned = pltpu.roll(jnp.where(low, under, top), 64, 1)
                    pair = jnp.where(same, straight, turned) * live
                    at = pl.ds(pl.multiple_of(t * 64, 64), 64)
                    outs[s][at, p * 128 : (p + 1) * 128] = pair.astype(jnp.bfloat16)
            return carry

        lax.fori_loop(0, count // batch, run, 0)

    for s in range(len(outs)):
        lay(s)


def pick(places, choose, raws, first, count, members):
    grid = len(raws)
    cols_dev, side2 = raws[0].shape[1:]
    total = count * members
    vmem = pl.BlockSpec(memory_space=pltpu.VMEM)
    shape = jax.ShapeDtypeStruct((count * 64, cols_dev * 64), jnp.bfloat16)
    return pl.pallas_call(
        functools.partial(pick_kernel, grid, first, count),
        out_shape=[shape] * members,
        in_specs=[pl.BlockSpec(memory_space=pltpu.SMEM), vmem]
        + [pl.BlockSpec(memory_space=pl.ANY)] * grid,
        out_specs=[vmem] * members,
        scratch_shapes=[
            pltpu.VMEM((total, cols_dev, side2), jnp.bfloat16),
            pltpu.SemaphoreType.DMA((total,)),
        ],
        compiler_params=pltpu.CompilerParams(vmem_limit_bytes=GRANT),
        cost_estimate=pl.CostEstimate(
            flops=0, transcendentals=0, bytes_accessed=4 * total * cols_dev * side2
        ),
        name="pick",
    )(places, choose, *raws)


def cut_kernel(widths, begin, wide, mask, b, *outs):
    blocks = mask.shape[0]
    shape = (mask.shape[1], b.shape[1])
    expand = (
        lax.broadcasted_iota(jnp.int32, shape, 1) // 64
        == lax.broadcasted_iota(jnp.int32, shape, 0)
    ).astype(jnp.float32)
    live = jnp.dot(
        mask[...].astype(jnp.float32), expand, preferred_element_type=jnp.float32
    ).astype(jnp.bfloat16)
    spans = [(sum(widths[:i]) + begin, w, outs[i]) for i, w in enumerate(widths)]
    if wide:
        spans = [(0, begin, None)] + spans
    for s in range(blocks):
        rows = slice(s * 64, (s + 1) * 64)
        for start, width, out in spans:
            cols = slice(start, start + width)
            kept = b[rows, cols] * live[s : s + 1, cols]
            if out is not None:
                out[rows, :] = kept
            if wide:
                outs[-1][rows, cols] = kept


def cut(b_matrix, b_mask, widths, begin, wide):
    vmem = pl.BlockSpec(memory_space=pltpu.VMEM)
    rows, full = b_matrix.shape
    read = full if wide else begin + sum(widths)
    outs = [*widths, full] if wide else widths

    def whole(shape):
        return pl.BlockSpec(shape, lambda i: (0, 0))

    return pl.pallas_call(
        functools.partial(cut_kernel, widths, begin, wide),
        grid=(1,),
        out_shape=[jax.ShapeDtypeStruct((rows, w), jnp.bfloat16) for w in outs],
        in_specs=[whole(b_mask.shape), whole((rows, read))],
        out_specs=[whole((rows, w)) for w in outs],
        cost_estimate=pl.CostEstimate(
            flops=0, transcendentals=0, bytes_accessed=6 * rows * read
        ),
        compiler_params=pltpu.CompilerParams(vmem_limit_bytes=GRANT),
        name="cut",
    )(b_mask, b_matrix)


def multiply_kernel(grid, planes_y, low, direct, spans, *refs):
    table = refs[0]
    count = grid * planes_y
    lefts = refs[1 : 1 + count]
    rights = [refs[1 + count * (i + 1) : 1 + count * (i + 2)] for i in range(len(spans))]
    outs = refs[1 + count * (1 + len(spans)) : -2]
    right, right_sems = refs[-2:]
    piece = lefts[0].shape[1]
    cols_dev = piece // 64
    width = right.shape[1]
    rows = lefts[0].shape[0] // 2
    step = tile_of(width)
    tiles = [(i, n * step) for i, (_, w) in enumerate(spans) for n in range(w // step)]
    for n, (i, at_span) in enumerate(tiles):
        for q in range(count):
            begin = at_span + (0 if q % planes_y else spans[i][0])
            for w in range(cols_dev):
                row = q * cols_dev + w
                code = table[row]
                at = pl.ds(pl.multiple_of(lax.bitwise_and(code, (1 << SHIFT) - 1), 64), 64)
                for o in range(grid):
                    @pl.when(lax.shift_right_logical(code, SHIFT) == o)
                    def _():
                        held = rights[i][o * planes_y + q % planes_y]
                        pltpu.make_async_copy(
                            held.at[at, begin : begin + step],
                            right.at[row * 64 : (row + 1) * 64, n * step : (n + 1) * step],
                            right_sems.at[n],
                        ).start()

    def run(n, carry):
        cols = pl.ds(pl.multiple_of(n * step, step), step)
        held = right.at[:, cols]
        pltpu.make_async_copy(held, held, right_sems.at[n]).wait()
        for g in (low, low + 1):
            same = slice((g - low) * rows, (g - low + 1) * rows)
            total = None
            for q in range(count):
                more = jnp.dot(
                    lefts[q][same, :],
                    right[q * piece : (q + 1) * piece, cols],
                    preferred_element_type=jnp.float32,
                )
                total = more if total is None else total + more
            if g < 2 and direct:
                put_code(outs[g], 0, cols, total)
            elif g < 2:
                outs[1][same, cols] = total
                put_code(outs[0], g * (rows + PAD), cols, total)
            elif g == 2:
                put_code(outs[0], 0, cols, total)
            else:
                outs[1][:, cols] = total
        return carry

    lax.fori_loop(0, width // step, run, 0)


def multiply(table, lefts, rights, low, direct, grid, planes_y, spans):
    part_rows, piece = lefts[0].shape
    rows = part_rows // 2
    inner = piece * len(lefts)
    width = sum(w for _, w in spans)
    tiles = width // tile_of(width)
    code = jax.ShapeDtypeStruct((rows + PAD, width), jnp.int16)
    if low == 0 and direct:
        outs = [code, code]
    elif low == 0:
        outs = [
            jax.ShapeDtypeStruct((2 * (rows + PAD), width), jnp.int16),
            jax.ShapeDtypeStruct((2 * rows, width), jnp.float32),
        ]
    else:
        outs = [code, jax.ShapeDtypeStruct((rows, width), jnp.float32)]
    hbm = pl.BlockSpec(memory_space=pl.ANY)
    vmem = pl.BlockSpec(memory_space=pltpu.VMEM)
    arrays = [v for span in rights for v in span]
    return pl.pallas_call(
        functools.partial(multiply_kernel, grid, planes_y, low, direct, spans),
        out_shape=outs,
        in_specs=[pl.BlockSpec(memory_space=pltpu.SMEM)]
        + [vmem] * len(lefts)
        + [hbm] * len(arrays),
        out_specs=[vmem] * 2,
        scratch_shapes=[
            pltpu.VMEM((inner, width), jnp.bfloat16),
            pltpu.SemaphoreType.DMA((tiles,)),
        ],
        compiler_params=pltpu.CompilerParams(vmem_limit_bytes=GRANT),
        cost_estimate=pl.CostEstimate(
            flops=2 * part_rows * inner * width,
            transcendentals=0,
            bytes_accessed=2 * inner * (part_rows + width) + 6 * part_rows * width,
        ),
        name="multiply",
    )(table, *lefts, *arrays)


def relay_kernel(own, code, three, two):
    rows = three.shape[0] - PAD

    def run(cols):
        total = own[0:rows, cols] + decode(code, rows + PAD, cols, rows)
        put_code(three, 0, cols, total)
        total = own[rows : 2 * rows, cols] + decode(code, 0, cols, rows)
        put_code(two, 0, cols, total)

    tiled(own.shape[1], run)


def relay(own, code):
    vmem = pl.BlockSpec(memory_space=pltpu.VMEM)
    out = jax.ShapeDtypeStruct((code.shape[0] // 2, code.shape[1]), code.dtype)
    return pl.pallas_call(
        relay_kernel,
        out_shape=[out, out],
        in_specs=[vmem, vmem],
        out_specs=[vmem, vmem],
        cost_estimate=pl.CostEstimate(
            flops=0, transcendentals=0, bytes_accessed=8 * own.size
        ),
        compiler_params=pltpu.CompilerParams(vmem_limit_bytes=GRANT),
        name="relay",
    )(own, code)


def finish_kernel(start, offset, own, three, two, one, *refs):
    out, stage, sem = refs[-3:]
    rows, width = stage.shape
    step = tile_of(width)

    def run(n, carry):
        cols = pl.ds(pl.multiple_of(n * step, step), step)
        wide = pl.ds(pl.multiple_of(offset + n * step, step), step)
        total = own[:, wide] + decode(one, 0, wide, rows)
        for code in (three, two):
            total = total + decode(code, 0, cols, rows)
        stage[:, cols] = total.astype(jnp.bfloat16)
        return carry

    lax.fori_loop(0, width // step, run, 0)
    copy = pltpu.make_async_copy(stage, out.at[:, start : start + width], sem)
    copy.start()
    copy.wait()


def finish(own, codes, start, offset, full, so_far):
    vmem = pl.BlockSpec(memory_space=pltpu.VMEM)
    hbm = pl.BlockSpec(memory_space=pl.ANY)
    operands = [own, *codes]
    specs = [vmem] * len(operands)
    rows, width = own.shape[0], codes[0].shape[1]
    aliases = {}
    if so_far is not None:
        aliases = {len(operands): 0}
        operands.append(so_far)
        specs.append(hbm)
    return pl.pallas_call(
        functools.partial(finish_kernel, start, offset),
        out_shape=jax.ShapeDtypeStruct((rows, full), jnp.bfloat16),
        in_specs=specs,
        out_specs=hbm,
        scratch_shapes=[pltpu.VMEM((rows, width), jnp.bfloat16), pltpu.SemaphoreType.DMA(())],
        input_output_aliases=aliases,
        compiler_params=pltpu.CompilerParams(vmem_limit_bytes=GRANT),
        cost_estimate=pl.CostEstimate(
            flops=0, transcendentals=0, bytes_accessed=12 * rows * width
        ),
        name="finish",
    )(*operands)


def body(a_blocks, a_mask, a_row_ids, a_col_ids, b_matrix, b_mask):
    grid = lax.axis_size("row")
    depth = lax.axis_size("depth")
    planes_y = depth // LINE
    rows_dev, cols_dev = a_blocks.shape[:2]
    home_rows = rows_dev // depth
    full = b_matrix.shape[1]
    unit = full // sum(CHUNKS)
    widths = [unit * c for c in CHUNKS]
    starts = [sum(widths[:j]) for j in range(len(widths))]

    my_row, my_col = lax.axis_index("row"), lax.axis_index("col")
    my_depth = lax.axis_index("depth")
    my_line, my_near = my_depth // planes_y, my_depth % planes_y
    n = jnp.arange(grid * planes_y * cols_dev, dtype=jnp.int32)
    piece = n // cols_dev
    holder = (my_col + piece // planes_y) % grid * depth
    holder = holder + my_line * planes_y + (my_near + piece % planes_y) % planes_y
    column = holder * cols_dev + n % cols_dev
    every = jnp.arange(a_col_ids.shape[0], dtype=jnp.int32)
    k = jnp.sum(jnp.where(every[None, :] == column[:, None], a_col_ids[None, :], 0), axis=1)
    shift = (k // (cols_dev * depth) - my_row + grid) % grid
    table = shift * (1 << SHIFT) + k % cols_dev * 64
    to = lax.broadcasted_iota(jnp.int32, (cols_dev * 64, cols_dev * 32), 0)
    come = lax.broadcasted_iota(jnp.int32, (cols_dev * 64, cols_dev * 32), 1)
    choose = (come == to % 64 // 2 * cols_dev + to // 64).astype(jnp.bfloat16)

    raws = [a_blocks] + [shifted(a_blocks, "row", o) for o in range(1, grid)]
    masks = [a_mask] + [shifted(a_mask, "row", o) for o in range(1, grid)]
    count = 2 * home_rows
    n = jnp.arange(4 * home_rows * planes_y, dtype=jnp.int32)
    low, rest = n // (count * planes_y) * 2, n % (count * planes_y)
    ahead = (rest // count + 1) % planes_y
    line = my_line ^ (LINE - 1 - low - rest % count // home_rows)
    block = (my_row * depth + line * planes_y + (my_near - ahead) % planes_y) * home_rows
    block = block + n % home_rows
    turned = lax.dynamic_slice(
        jnp.concatenate([a_row_ids, a_row_ids]), (my_row * rows_dev,), a_row_ids.shape
    )
    bits = jnp.concatenate(masks) << jnp.arange(cols_dev, dtype=jnp.int32)[None, :]
    entry = jnp.arange(grid * rows_dev, dtype=jnp.int32) + SLOTS * jnp.sum(bits, axis=1)
    places = jnp.sum(jnp.where(turned[None, :] == block[:, None], entry[None, :], 0), axis=1)
    early = cut(b_matrix, b_mask, widths[:1], 0, False)
    *later, whole = cut(b_matrix, b_mask, widths[1:], widths[0], True)
    cuts = [*early, *later]
    wholes = [whole] + [shifted(whole, "row", o) for o in range(1, grid)]

    parts = []
    for n in range(2):
        first = n * count * planes_y
        picked = list(pick(places, choose, raws, first, count, planes_y - 1))
        first += count * (planes_y - 1)
        near = list(pick(places, choose, raws, first, count, 1)) + picked
        near = [member(v, planes_y, s) if s else v for s, v in enumerate(near)]
        far = []
        for x in range(1, grid):
            for v in near:
                far.append(shifted(v, "col", x))
        parts.append(near + far)

    rights, far = [], []
    for j, (start, width, mine) in enumerate(zip(starts, widths, cuts)):
        direct = j < DIRECT
        near = [member(mine, planes_y, s) for s in range(1, planes_y)]
        held = [wholes[0]] + near
        for o in range(1, grid):
            held += [wholes[o]] + [shifted(v, "row", o) for v in near]
        rights.append(held)
        spans = ((start, width),)
        first, second = multiply(table, parts[0], [held], 0, direct, grid, planes_y, spans)
        if direct:
            three = hop(first, planes_y, ALL, 3)
            two = hop(second, planes_y, ALL, 2)
        else:
            came = hop(first, planes_y, EDGES, 1)
            three, two = relay(second, came)
            three = hop(three, planes_y, INNER, 3)
            two = hop(two, planes_y, INNER, 2)
        far.append((three, two))

    product = None
    for chunks in NEAR:
        spans = tuple((starts[j], widths[j]) for j in chunks)
        held = [rights[j] for j in chunks]
        code, own = multiply(table, parts[1], held, 2, False, grid, planes_y, spans)
        one = hop(code, planes_y, ALL, 1)
        for j in chunks:
            offset = starts[j] - starts[chunks[0]]
            codes = [*far[j], one]
            product = finish(own, codes, starts[j], offset, full, product)
    return product


def solution(mesh):
    return jax.shard_map(
        body,
        mesh=mesh,
        in_specs=(
            P("row", ("col", "depth"), None),
            P("row", ("col", "depth")),
            P(),
            P(),
            P(("row", "depth"), "col"),
            P(("row", "depth"), "col"),
        ),
        out_specs=P(("row", "depth"), "col"),
        check_vma=False,
    )
```

```python
import functools
import math

import jax
import jax.numpy as jnp
from jax import lax
from jax.experimental import pallas as pl
from jax.experimental.pallas import tpu as pltpu
from jax.sharding import PartitionSpec as P


LINE = 4
CHUNKS = (3, 3, 3, 2, 1)
DIRECT = 2
NEAR = ((0,), (1,), (2,), (3, 4))
SPAN = 32760.0
PAD = 8
SHIFT = 16
GRANT = 24 << 20
SLOTS = 64


def shifted(value, axis, offset):
    size = lax.axis_size(axis)
    return lax.ppermute(value, axis, [((i + offset) % size, i) for i in range(size)])


def member(value, near, offset):
    planes = lax.axis_size("depth") // near
    pairs = [
        (z * near + (y + offset) % near, z * near + y) for z in range(planes) for y in range(near)
    ]
    return lax.ppermute(value, "depth", pairs)


def hop(value, near, senders, flip):
    pairs = [(z * near + y, (z ^ flip) * near + y) for z in senders for y in range(near)]
    return lax.ppermute(value, "depth", pairs)


ALL = tuple(range(LINE))
EDGES = (0, LINE - 1)
INNER = tuple(range(1, LINE - 1))


def encode(total):
    peak = jnp.max(jnp.abs(total), axis=0, keepdims=True)
    level = jnp.ceil(jnp.log2(jnp.maximum(peak, 1e-30)) * 16.0)
    scaled = total * (jnp.exp2(level * (-1.0 / 16.0)) * SPAN)
    return jnp.round(scaled).astype(jnp.int32).astype(jnp.int16), level


def put_code(ref, at, cols, total):
    code, level = encode(total)
    rows = total.shape[0]
    ref[at : at + rows, cols] = code
    ref[at + rows : at + rows + PAD, cols] = (
        jnp.broadcast_to(level, (PAD, level.shape[1])).astype(jnp.int32).astype(jnp.int16)
    )


def decode(ref, at, cols, rows):
    level = ref[at + rows : at + rows + PAD, cols].astype(jnp.int32).astype(jnp.float32)[0:1]
    return ref[at : at + rows, cols].astype(jnp.int32).astype(jnp.float32) * (
        jnp.exp2(level * (1.0 / 16.0)) * (1.0 / SPAN)
    )


def tile_of(width):
    return 256 if width % 256 == 0 else 128


def tiled(width, fn):
    step = tile_of(width)

    def run(n, carry):
        fn(pl.ds(pl.multiple_of(n * step, step), step))
        return carry

    lax.fori_loop(0, width // step, run, 0)


def pick_kernel(grid, first, count, *refs):
    places, choose = refs[0], refs[1]
    raws = refs[2 : 2 + grid]
    outs = refs[2 + grid : -2]
    held, sems = refs[-2:]
    rows_dev, cols_dev = raws[0].shape[0], raws[0].shape[1]
    batch = math.gcd(count, 4)
    total = count * len(outs)

    def fetch(n, carry):
        slot = lax.bitwise_and(places[first + n], SLOTS - 1)
        for o in range(grid):
            @pl.when(lax.div(slot, rows_dev) == o)
            def _():
                held_row = raws[o].at[lax.rem(slot, rows_dev)]
                pltpu.make_async_copy(held_row, held.at[n], sems.at[n]).start()
        return carry

    lax.fori_loop(0, total, fetch, 0)
    low = lax.broadcasted_iota(jnp.int32, (64, 128), 1) < 64
    even = lax.broadcasted_iota(jnp.int32, (64, 128), 0) % 2 == 0
    same = low == even
    low_row = lax.broadcasted_iota(jnp.int32, (1, 128), 1) < 64

    def lay(s):
        def run(m, carry):
            stored = []
            for h in range(batch):
                n = s * count + m * batch + h
                pltpu.make_async_copy(raws[0].at[0], held.at[n], sems.at[n]).wait()
                x = held[n].astype(jnp.float32)
                parts = [x[:, 128 * i : 128 * (i + 1)] for i in range(32)]
                stored.append(jnp.concatenate(parts, axis=0).astype(jnp.bfloat16))
            spread = jnp.dot(
                choose[...],
                jnp.concatenate(stored, axis=1),
                preferred_element_type=jnp.float32,
            )
            for h in range(batch):
                t = m * batch + h
                place = places[first + s * count + t]
                for p in range(cols_dev // 2):
                    bit = jnp.where(low_row, SLOTS << (2 * p), SLOTS << (2 * p + 1))
                    live = (lax.bitwise_and(bit, place) != 0).astype(jnp.float32)
                    lanes = slice(128 * h, 128 * (h + 1))
                    top = spread[2 * p * 64 : (2 * p + 1) * 64, lanes]
                    under = spread[(2 * p + 1) * 64 : (2 * p + 2) * 64, lanes]
                    straight = jnp.where(low, top, under)
                    turned = pltpu.roll(jnp.where(low, under, top), 64, 1)
                    pair = jnp.where(same, straight, turned) * live
                    at = pl.ds(pl.multiple_of(t * 64, 64), 64)
                    outs[s][at, p * 128 : (p + 1) * 128] = pair.astype(jnp.bfloat16)
            return carry

        lax.fori_loop(0, count // batch, run, 0)

    for s in range(len(outs)):
        lay(s)


def pick(places, choose, raws, first, count, members):
    grid = len(raws)
    cols_dev, side2 = raws[0].shape[1:]
    total = count * members
    vmem = pl.BlockSpec(memory_space=pltpu.VMEM)
    shape = jax.ShapeDtypeStruct((count * 64, cols_dev * 64), jnp.bfloat16)
    return pl.pallas_call(
        functools.partial(pick_kernel, grid, first, count),
        out_shape=[shape] * members,
        in_specs=[pl.BlockSpec(memory_space=pltpu.SMEM), vmem]
        + [pl.BlockSpec(memory_space=pl.ANY)] * grid,
        out_specs=[vmem] * members,
        scratch_shapes=[
            pltpu.VMEM((total, cols_dev, side2), jnp.bfloat16),
            pltpu.SemaphoreType.DMA((total,)),
        ],
        compiler_params=pltpu.CompilerParams(vmem_limit_bytes=GRANT),
        cost_estimate=pl.CostEstimate(
            flops=0, transcendentals=0, bytes_accessed=4 * total * cols_dev * side2
        ),
        name="pick",
    )(places, choose, *raws)


def cut_kernel(widths, begin, wide, mask, b, *outs):
    blocks = mask.shape[0]
    shape = (mask.shape[1], b.shape[1])
    expand = (
        lax.broadcasted_iota(jnp.int32, shape, 1) // 64
        == lax.broadcasted_iota(jnp.int32, shape, 0)
    ).astype(jnp.float32)
    live = jnp.dot(
        mask[...].astype(jnp.float32), expand, preferred_element_type=jnp.float32
    ).astype(jnp.bfloat16)
    spans = [(sum(widths[:i]) + begin, w, outs[i]) for i, w in enumerate(widths)]
    if wide:
        spans = [(0, begin, None)] + spans
    for s in range(blocks):
        rows = slice(s * 64, (s + 1) * 64)
        for start, width, out in spans:
            cols = slice(start, start + width)
            kept = b[rows, cols] * live[s : s + 1, cols]
            if out is not None:
                out[rows, :] = kept
            if wide:
                outs[-1][rows, cols] = kept


def cut(b_matrix, b_mask, widths, begin, wide):
    vmem = pl.BlockSpec(memory_space=pltpu.VMEM)
    rows, full = b_matrix.shape
    read = full if wide else begin + sum(widths)
    outs = [*widths, full] if wide else widths

    def whole(shape):
        return pl.BlockSpec(shape, lambda i: (0, 0))

    return pl.pallas_call(
        functools.partial(cut_kernel, widths, begin, wide),
        grid=(1,),
        out_shape=[jax.ShapeDtypeStruct((rows, w), jnp.bfloat16) for w in outs],
        in_specs=[whole(b_mask.shape), whole((rows, read))],
        out_specs=[whole((rows, w)) for w in outs],
        cost_estimate=pl.CostEstimate(
            flops=0, transcendentals=0, bytes_accessed=6 * rows * read
        ),
        compiler_params=pltpu.CompilerParams(vmem_limit_bytes=GRANT),
        name="cut",
    )(b_mask, b_matrix)


def multiply_kernel(grid, planes_y, low, direct, spans, *refs):
    table = refs[0]
    count = grid * planes_y
    lefts = refs[1 : 1 + count]
    rights = [refs[1 + count * (i + 1) : 1 + count * (i + 2)] for i in range(len(spans))]
    outs = refs[1 + count * (1 + len(spans)) : -2]
    right, right_sems = refs[-2:]
    piece = lefts[0].shape[1]
    cols_dev = piece // 64
    width = right.shape[1]
    rows = lefts[0].shape[0] // 2
    step = tile_of(width)
    tiles = [(i, n * step) for i, (_, w) in enumerate(spans) for n in range(w // step)]
    for n, (i, at_span) in enumerate(tiles):
        for q in range(count):
            begin = at_span + (0 if q % planes_y else spans[i][0])
            for w in range(cols_dev):
                row = q * cols_dev + w
                code = table[row]
                at = pl.ds(pl.multiple_of(lax.bitwise_and(code, (1 << SHIFT) - 1), 64), 64)
                for o in range(grid):
                    @pl.when(lax.shift_right_logical(code, SHIFT) == o)
                    def _():
                        held = rights[i][o * planes_y + q % planes_y]
                        pltpu.make_async_copy(
                            held.at[at, begin : begin + step],
                            right.at[row * 64 : (row + 1) * 64, n * step : (n + 1) * step],
                            right_sems.at[n],
                        ).start()

    def run(n, carry):
        cols = pl.ds(pl.multiple_of(n * step, step), step)
        held = right.at[:, cols]
        pltpu.make_async_copy(held, held, right_sems.at[n]).wait()
        for g in (low, low + 1):
            same = slice((g - low) * rows, (g - low + 1) * rows)
            total = None
            for q in range(count):
                more = jnp.dot(
                    lefts[q][same, :],
                    right[q * piece : (q + 1) * piece, cols],
                    preferred_element_type=jnp.float32,
                )
                total = more if total is None else total + more
            if g < 2 and direct:
                put_code(outs[g], 0, cols, total)
            elif g < 2:
                outs[1][same, cols] = total
                put_code(outs[0], g * (rows + PAD), cols, total)
            elif g == 2:
                put_code(outs[0], 0, cols, total)
            else:
                outs[1][:, cols] = total
        return carry

    lax.fori_loop(0, width // step, run, 0)


def multiply(table, lefts, rights, low, direct, grid, planes_y, spans):
    part_rows, piece = lefts[0].shape
    rows = part_rows // 2
    inner = piece * len(lefts)
    width = sum(w for _, w in spans)
    tiles = width // tile_of(width)
    code = jax.ShapeDtypeStruct((rows + PAD, width), jnp.int16)
    if low == 0 and direct:
        outs = [code, code]
    elif low == 0:
        outs = [
            jax.ShapeDtypeStruct((2 * (rows + PAD), width), jnp.int16),
            jax.ShapeDtypeStruct((2 * rows, width), jnp.float32),
        ]
    else:
        outs = [code, jax.ShapeDtypeStruct((rows, width), jnp.float32)]
    hbm = pl.BlockSpec(memory_space=pl.ANY)
    vmem = pl.BlockSpec(memory_space=pltpu.VMEM)
    arrays = [v for span in rights for v in span]
    return pl.pallas_call(
        functools.partial(multiply_kernel, grid, planes_y, low, direct, spans),
        out_shape=outs,
        in_specs=[pl.BlockSpec(memory_space=pltpu.SMEM)]
        + [vmem] * len(lefts)
        + [hbm] * len(arrays),
        out_specs=[vmem] * 2,
        scratch_shapes=[
            pltpu.VMEM((inner, width), jnp.bfloat16),
            pltpu.SemaphoreType.DMA((tiles,)),
        ],
        compiler_params=pltpu.CompilerParams(vmem_limit_bytes=GRANT),
        cost_estimate=pl.CostEstimate(
            flops=2 * part_rows * inner * width,
            transcendentals=0,
            bytes_accessed=2 * inner * (part_rows + width) + 6 * part_rows * width,
        ),
        name="multiply",
    )(table, *lefts, *arrays)


def relay_kernel(own, code, three, two):
    rows = three.shape[0] - PAD

    def run(cols):
        total = own[0:rows, cols] + decode(code, rows + PAD, cols, rows)
        put_code(three, 0, cols, total)
        total = own[rows : 2 * rows, cols] + decode(code, 0, cols, rows)
        put_code(two, 0, cols, total)

    tiled(own.shape[1], run)


def relay(own, code):
    vmem = pl.BlockSpec(memory_space=pltpu.VMEM)
    out = jax.ShapeDtypeStruct((code.shape[0] // 2, code.shape[1]), code.dtype)
    return pl.pallas_call(
        relay_kernel,
        out_shape=[out, out],
        in_specs=[vmem, vmem],
        out_specs=[vmem, vmem],
        cost_estimate=pl.CostEstimate(
            flops=0, transcendentals=0, bytes_accessed=8 * own.size
        ),
        compiler_params=pltpu.CompilerParams(vmem_limit_bytes=GRANT),
        name="relay",
    )(own, code)


def finish_kernel(start, offset, own, three, two, one, *refs):
    out, stage, sem = refs[-3:]
    rows, width = stage.shape
    step = tile_of(width)

    def run(n, carry):
        cols = pl.ds(pl.multiple_of(n * step, step), step)
        wide = pl.ds(pl.multiple_of(offset + n * step, step), step)
        total = own[:, wide] + decode(one, 0, wide, rows)
        for code in (three, two):
            total = total + decode(code, 0, cols, rows)
        stage[:, cols] = total.astype(jnp.bfloat16)
        return carry

    lax.fori_loop(0, width // step, run, 0)
    copy = pltpu.make_async_copy(stage, out.at[:, start : start + width], sem)
    copy.start()
    copy.wait()


def finish(own, codes, start, offset, full, so_far):
    vmem = pl.BlockSpec(memory_space=pltpu.VMEM)
    hbm = pl.BlockSpec(memory_space=pl.ANY)
    operands = [own, *codes]
    specs = [vmem] * len(operands)
    rows, width = own.shape[0], codes[0].shape[1]
    aliases = {}
    if so_far is not None:
        aliases = {len(operands): 0}
        operands.append(so_far)
        specs.append(hbm)
    return pl.pallas_call(
        functools.partial(finish_kernel, start, offset),
        out_shape=jax.ShapeDtypeStruct((rows, full), jnp.bfloat16),
        in_specs=specs,
        out_specs=hbm,
        scratch_shapes=[pltpu.VMEM((rows, width), jnp.bfloat16), pltpu.SemaphoreType.DMA(())],
        input_output_aliases=aliases,
        compiler_params=pltpu.CompilerParams(vmem_limit_bytes=GRANT),
        cost_estimate=pl.CostEstimate(
            flops=0, transcendentals=0, bytes_accessed=12 * rows * width
        ),
        name="finish",
    )(*operands)


def body(a_blocks, a_mask, a_row_ids, a_col_ids, b_matrix, b_mask):
    grid = lax.axis_size("row")
    depth = lax.axis_size("depth")
    planes_y = depth // LINE
    rows_dev, cols_dev = a_blocks.shape[:2]
    home_rows = rows_dev // depth
    full = b_matrix.shape[1]
    unit = full // sum(CHUNKS)
    widths = [unit * c for c in CHUNKS]
    starts = [sum(widths[:j]) for j in range(len(widths))]

    my_row, my_col = lax.axis_index("row"), lax.axis_index("col")
    my_depth = lax.axis_index("depth")
    my_line, my_near = my_depth // planes_y, my_depth % planes_y
    n = jnp.arange(grid * planes_y * cols_dev, dtype=jnp.int32)
    piece = n // cols_dev
    holder = (my_col + piece // planes_y) % grid * depth
    holder = holder + my_line * planes_y + (my_near + piece % planes_y) % planes_y
    column = holder * cols_dev + n % cols_dev
    every = jnp.arange(a_col_ids.shape[0], dtype=jnp.int32)
    k = jnp.sum(jnp.where(every[None, :] == column[:, None], a_col_ids[None, :], 0), axis=1)
    shift = (k // (cols_dev * depth) - my_row + grid) % grid
    table = shift * (1 << SHIFT) + k % cols_dev * 64
    to = lax.broadcasted_iota(jnp.int32, (cols_dev * 64, cols_dev * 32), 0)
    come = lax.broadcasted_iota(jnp.int32, (cols_dev * 64, cols_dev * 32), 1)
    choose = (come == to % 64 // 2 * cols_dev + to // 64).astype(jnp.bfloat16)

    raws = [a_blocks] + [shifted(a_blocks, "row", o) for o in range(1, grid)]
    masks = [a_mask] + [shifted(a_mask, "row", o) for o in range(1, grid)]
    count = 2 * home_rows
    n = jnp.arange(4 * home_rows * planes_y, dtype=jnp.int32)
    low, rest = n // (count * planes_y) * 2, n % (count * planes_y)
    ahead = (rest // count + 1) % planes_y
    line = my_line ^ (LINE - 1 - low - rest % count // home_rows)
    block = (my_row * depth + line * planes_y + (my_near - ahead) % planes_y) * home_rows
    block = block + n % home_rows
    turned = lax.dynamic_slice(
        jnp.concatenate([a_row_ids, a_row_ids]), (my_row * rows_dev,), a_row_ids.shape
    )
    bits = jnp.concatenate(masks) << jnp.arange(cols_dev, dtype=jnp.int32)[None, :]
    entry = jnp.arange(grid * rows_dev, dtype=jnp.int32) + SLOTS * jnp.sum(bits, axis=1)
    places = jnp.sum(jnp.where(turned[None, :] == block[:, None], entry[None, :], 0), axis=1)
    early = cut(b_matrix, b_mask, widths[:1], 0, False)
    *later, whole = cut(b_matrix, b_mask, widths[1:], widths[0], True)
    cuts = [*early, *later]
    wholes = [whole] + [shifted(whole, "row", o) for o in range(1, grid)]

    parts = []
    for n in range(2):
        first = n * count * planes_y
        picked = list(pick(places, choose, raws, first, count, planes_y - 1))
        first += count * (planes_y - 1)
        near = list(pick(places, choose, raws, first, count, 1)) + picked
        near = [member(v, planes_y, s) if s else v for s, v in enumerate(near)]
        far = []
        for x in range(1, grid):
            for v in near:
                far.append(shifted(v, "col", x))
        parts.append(near + far)

    rights, far = [], []
    for j, (start, width, mine) in enumerate(zip(starts, widths, cuts)):
        direct = j < DIRECT
        near = [member(mine, planes_y, s) for s in range(1, planes_y)]
        held = [wholes[0]] + near
        for o in range(1, grid):
            held += [wholes[o]] + [shifted(v, "row", o) for v in near]
        rights.append(held)
        spans = ((start, width),)
        first, second = multiply(table, parts[0], [held], 0, direct, grid, planes_y, spans)
        if direct:
            three = hop(first, planes_y, ALL, 3)
            two = hop(second, planes_y, ALL, 2)
        else:
            came = hop(first, planes_y, EDGES, 1)
            three, two = relay(second, came)
            three = hop(three, planes_y, INNER, 3)
            two = hop(two, planes_y, INNER, 2)
        far.append((three, two))

    product = None
    for chunks in NEAR:
        spans = tuple((starts[j], widths[j]) for j in chunks)
        held = [rights[j] for j in chunks]
        code, own = multiply(table, parts[1], held, 2, False, grid, planes_y, spans)
        one = hop(code, planes_y, ALL, 1)
        for j in chunks:
            offset = starts[j] - starts[chunks[0]]
            codes = [*far[j], one]
            product = finish(own, codes, starts[j], offset, full, product)
    return product


def solution(mesh):
    return jax.shard_map(
        body,
        mesh=mesh,
        in_specs=(
            P("row", ("col", "depth"), None),
            P("row", ("col", "depth")),
            P(),
            P(),
            P(("row", "depth"), "col"),
            P(("row", "depth"), "col"),
        ),
        out_specs=P(("row", "depth"), "col"),
        check_vma=False,
    )
```
